512 devices in a mesh: grp: 32 (over z, x), vox: 16 (over y, core).
Axes of the slice: x: 4, y: 8, z: 8, core: 2. Of those that a mesh axis runs over, the one named last changes fastest.
Arguments:
- group_basis: bfloat16 [32, 16384, 256], P('grp', 'vox'), may hold values from -6 to 6
- timeseries: bfloat16 [32, 16384, 512], P('grp', 'vox'), may hold values from -6 to 6
Outputs:
- loadings: float32 [32, 256, 512], P('grp', 'vox')
The draws below stay inside these ranges and needn't reach their ends.
All inputs are finite; a program needn't handle non-finite values.
Results may differ from the reference program's by a relative error of at most 0.015.
Values may be sent and summed in bfloat16 or wider, within the bound.
No kernel may reach another device: no remote copies, remote signals or barrier semaphores. Data moves between devices by JAX's collectives and lax.ppermute only.
A program may use at most 64 MiB of HBM per device.

```python
import jax
import jax.numpy as jnp
from jax import lax

COMPONENTS = 256
FRAMES = 512
LEVELS = 3
ITERS = 2
GROUPS = 32
VOXELS = 16384


def shard_levels(rng, shape, split, least, high):
    level = 1.0
    for dim, shards_of in split:
        draws = jax.random.uniform(jax.random.fold_in(jax.random.fold_in(rng, 6), dim), (shards_of,), jnp.float32, least / len(split), high / len(split))
        level = level * jnp.repeat(jnp.exp(draws), shape[dim] // shards_of).reshape((-1,) + (1,) * (len(shape) - 1 - dim))
    return level


def scatter_about(stream_key, extent, deviation, reach, split=(), kind=jnp.bfloat16):
    loudness = shard_levels(stream_key, extent, split, -0.22, 0.18) if split else 1.0
    entries = jax.random.normal(stream_key, extent, jnp.float32) * deviation * loudness
    return jnp.minimum(jnp.maximum(entries, -reach), reach).astype(kind)


def setup_inputs(seed: int = 0) -> dict:
    streams_of = jax.random.split(jax.random.key(seed), 3)
    group_basis = scatter_about(streams_of[0], (GROUPS, VOXELS, COMPONENTS), 1.0, 6.0, ((0, 32), (1, 16)))
    timeseries = scatter_about(streams_of[1], (GROUPS, VOXELS, FRAMES), 1.0, 6.0, ((0, 32), (1, 16)))
    return dict(group_basis=group_basis, timeseries=timeseries)


def gram_block(left_side, right_side):
    return lax.dot_general(left_side.astype(jnp.float32), right_side.astype(jnp.float32), (((0,), (0,)), ((), ())), preferred_element_type=jnp.float32)

def merge_pair(first_basis, second_basis):
    stacked = jnp.concatenate([first_basis, second_basis], axis=1)
    gram_matrix = gram_block(stacked, stacked)
    identity = jnp.eye(COMPONENTS, dtype=jnp.float32)
    weights = jnp.concatenate([identity, identity], axis=0)
    for sweep_idx in range(ITERS):
        imaged = jnp.dot(gram_matrix, weights, precision=lax.Precision.HIGHEST)
        curved = jnp.dot(gram_matrix, imaged, precision=lax.Precision.HIGHEST)
        inner_gram = jnp.dot(imaged.T, curved, precision=lax.Precision.HIGHEST)
        factor = jnp.linalg.cholesky(inner_gram)
        weights = lax.linalg.triangular_solve(factor, imaged, left_side=False, lower=True, transpose_a=True)
    merged = jnp.dot(stacked.astype(jnp.float32), weights.astype(jnp.bfloat16).astype(jnp.float32), preferred_element_type=jnp.float32)
    return merged.astype(jnp.bfloat16)

def merge_node_pair(node_pair):
    return merge_pair(node_pair[0], node_pair[1])

def project_block(item_pair):
    root_basis, series_block = item_pair
    group_span = series_block.shape[0]
    flattened = jnp.transpose(series_block, (1, 0, 2)).reshape(VOXELS, group_span * FRAMES)
    projected = gram_block(root_basis, flattened)
    return jnp.transpose(projected.reshape(COMPONENTS, group_span, FRAMES), (1, 0, 2))

def reference(group_basis, timeseries):
    tree_nodes = group_basis
    for level_idx in range(LEVELS):
        pair_count = tree_nodes.shape[0] // 2
        node_pairs = tree_nodes.reshape(pair_count, 2, VOXELS, COMPONENTS)
        tree_nodes = lax.map(merge_node_pair, node_pairs)
    root_count = tree_nodes.shape[0]
    series_blocks = timeseries.reshape(root_count, GROUPS // root_count, VOXELS, FRAMES)
    result = lax.map(project_block, (tree_nodes, series_blocks))
    return result.reshape(GROUPS, COMPONENTS, FRAMES)
```

```python
import functools

import jax
import jax.numpy as jnp
from jax import lax
from jax.experimental import pallas as pl
from jax.experimental.pallas import tpu as pltpu
from jax.sharding import PartitionSpec as P

N = 256
VOX = 16
ROWS = N // VOX
F32 = jnp.float32
BF16 = jnp.bfloat16

NN = (((1,), (0,)), ((), ()))
NT = (((1,), (1,)), ((), ()))
TN = (((0,), (0,)), ((), ()))


def dot1(a, b, dims):
    return lax.dot_general(a.astype(BF16), b.astype(BF16), dims, preferred_element_type=F32)


def split(x):
    hi = x.astype(BF16)
    return hi, (x - hi.astype(F32)).astype(BF16)


def dot3(a, b, dims):
    dot = functools.partial(lax.dot_general, dimension_numbers=dims, preferred_element_type=F32)
    return dot(a[0], b[0]) + (dot(a[0], b[1]) + dot(a[1], b[0]))


def dot_full(a, b, dims):
    return lax.dot_general(a, b, dims, preferred_element_type=F32, precision=lax.Precision.HIGHEST)


def iotas():
    shape = (N, N)
    return lax.broadcasted_iota(jnp.int32, shape, 0), lax.broadcasted_iota(jnp.int32, shape, 1)


def inv_sqrt_diag(m, eye):
    picked = jnp.where(eye, m, 0.0)
    col = lax.rsqrt(jnp.sum(picked, axis=1, keepdims=True))
    row = lax.rsqrt(jnp.sum(picked, axis=0, keepdims=True))
    return col, row


def inverse_factor_fast(m):
    r, c = iotas()
    eye = r == c
    below = r > c
    one = jnp.where(eye, 1.0, 0.0)
    col, row = inv_sqrt_diag(m, eye)
    m = col * m * row
    start = row
    s = jnp.where(below, m, 0.0)
    s2 = dot1(s, s, NN)
    t = one - s
    x = t + dot1(t, s2, NN)
    for _ in range(2):
        mk = dot1(dot1(x, m, NN), x, NT)
        col, row = inv_sqrt_diag(mk, eye)
        s = jnp.where(below, col * mk * row, 0.0)
        s2 = dot1(s, s, NN)
        t = one - s
        x = col * x
        x = x - dot1(s, x, NN) + dot1(dot1(t, s2, NN), x, NN)
    x = jnp.where(r >= c, x, 0.0)
    xs = split(x)
    mk = dot3(split(dot3(xs, split(m), NN)), xs, NT)
    col, row = inv_sqrt_diag(mk, eye)
    off = jnp.where(eye, 0.0, col * mk * row)
    size = jnp.sum(off * off)
    s = jnp.where(below, off, 0.0)
    x = col * x
    step = s - dot1(s, s, NN)
    x = x - dot3(split(step), split(x), NN)
    return x * start, size


def factor_exact(m_ref, l_ref):
    r, c = iotas()

    def body(j, _):
        m = m_ref[...]
        row = jnp.sum(jnp.where(r == j, m, 0.0), axis=0, keepdims=True)
        col = jnp.sum(jnp.where(c == j, m, 0.0), axis=1, keepdims=True)
        pivot = jnp.sum(jnp.where((r == j) & (c == j), m, 0.0))
        row = jnp.where(c[:1] >= j, row, 0.0)
        col = jnp.where(r[:, :1] >= j, col, 0.0)
        m_ref[...] = m - col * (row / pivot)
        scale = jnp.full((1, N), pivot, F32)
        l_ref[...] = jnp.where(c == j, col / jnp.sqrt(scale), l_ref[...])
        return 0

    lax.fori_loop(0, N, body, 0)


def invert_lower(l):
    r, c = iotas()
    eye = r == c
    diag = jnp.sum(jnp.where(eye, l, 0.0), axis=1, keepdims=True)
    x = jnp.where(eye, 1.0 / diag, 0.0)
    size = 1
    while size < N:
        off = jnp.where((r // (2 * size) == c // (2 * size)) & (r // size > c // size), l, 0.0)
        x = x - dot_full(dot_full(x, off, NN), x, NN)
        size *= 2
    return x


def pair(a0, a1, b0, b1, d0, d1):
    return dot3(a0, b0, d0) + dot3(a1, b1, d1)


def merge_kernel(plain, sec_ref, aa_ref, c_ref, own_ref, other_ref, out_ref, wt_ref, m_ref, l_ref):
    cross = c_ref[...].astype(F32)
    if plain:
        r, c = iotas()
        one = jnp.where(r == c, 1.0, 0.0)
        cs = split(cross)
        t0, t1 = one + cross.T, one + cross

        def times(t0, t1):
            s0, s1 = split(t0), split(t1)
            return t0 + dot3(s1, cs, NT), dot3(s0, cs, NN) + t1

        unscale = 1.0
    else:
        sec = sec_ref[0]
        a, b = aa_ref[sec], aa_ref[1 - sec]
        r, c = iotas()
        top = jnp.max(jnp.where(r == c, jnp.maximum(a, b), 0.0))
        top = jnp.full((1, N), top, F32)
        inv = 1.0 / top
        unscale = lax.rsqrt(top)
        a, b, cross = a * inv, b * inv, cross * inv
        pa, pb, cs = split(a), split(b), split(cross)
        t0, t1 = a + cross.T, b + cross

        def times(t0, t1):
            s0, s1 = split(t0), split(t1)
            return pair(s0, s1, pa, cs, NN, NT), pair(s0, s1, cs, pb, NN, NN)

    u0, u1 = times(t0, t1)
    v0, v1 = times(u0, u1)
    us0, us1 = split(u0), split(u1)
    m = dot3(split(v0), us0, NT) + dot3(split(v1), us1, NT)
    x, size = inverse_factor_fast(m)
    xs = split(x)
    wt_ref[0] = dot3(xs, us0, NN) * unscale
    wt_ref[1] = dot3(xs, us1, NN) * unscale
    good = size < 0.01

    @pl.when(jnp.logical_not(good))
    def _():
        y0, y1 = t0, t1
        for it in range(2):
            if plain:
                z0 = y0 + dot_full(y1, cross, NT)
                z1 = dot_full(y0, cross, NN) + y1
            else:
                z0 = dot_full(y0, a, NN) + dot_full(y1, cross, NT)
                z1 = dot_full(y0, cross, NN) + dot_full(y1, b, NN)
            m_ref[...] = dot_full(z0, y0, NT) + dot_full(z1, y1, NT)
            l_ref[...] = jnp.zeros((N, N), F32)
            factor_exact(m_ref, l_ref)
            xi = invert_lower(l_ref[...])
            if it == 0:
                y0, y1 = dot_full(xi, z0, NN), dot_full(xi, z1, NN)
            else:
                wt_ref[0] = dot_full(xi, y0, NN) * unscale
                wt_ref[1] = dot_full(xi, y1, NN) * unscale

    out = dot1(own_ref[...], wt_ref[0], NT) + dot1(other_ref[...], wt_ref[1], NT)
    out_ref[...] = out.astype(BF16)


def merge(sec, aa, cross, own, other):
    plain = aa is None
    rows = own.shape[0]
    vmem = pl.BlockSpec(memory_space=pltpu.VMEM)
    args = [sec, cross if plain else aa, cross, own, other]
    body = functools.partial(merge_kernel, plain)
    return pl.pallas_call(
        body,
        out_shape=jax.ShapeDtypeStruct((rows, N), BF16),
        in_specs=[pl.BlockSpec(memory_space=pltpu.SMEM), vmem, vmem, vmem, vmem],
        out_specs=vmem,
        scratch_shapes=[pltpu.VMEM((2, N, N), F32), pltpu.VMEM((N, N), F32), pltpu.VMEM((N, N), F32)],
        compiler_params=pltpu.CompilerParams(vmem_limit_bytes=48 << 20),
        name="merge_plain" if plain else "merge_full",
    )(*args)


def gram(a, b):
    return lax.dot_general(a, b, TN, preferred_element_type=F32)


def partner(value, mask):
    return lax.ppermute(value, "grp", [(g, g ^ mask) for g in range(32)])


def shared_groups(mask):
    firsts = [g for g in range(32) if not g & mask]
    return [[h * VOX + v for h in (g, g | mask) for v in range(VOX)] for g in firsts]


def scatter_sum(value, dtype):
    parts = value.astype(dtype).reshape((VOX, value.shape[0] // VOX) + value.shape[1:])
    parts = lax.all_to_all(parts, "vox", 0, 0)
    return jnp.sum(parts.astype(F32), axis=0)


def collect(rows, dtype):
    sent = jnp.broadcast_to(rows.astype(dtype)[None], (VOX,) + rows.shape)
    return lax.all_to_all(sent, "vox", 0, 0).reshape((-1,) + rows.shape[1:])


def local(group_basis, timeseries):
    current = group_basis[0]
    series = timeseries[0]
    position = lax.axis_index("grp")
    sec = (position & 1).astype(jnp.int32).reshape(1)
    other = partner(current, 1)
    own_rows = scatter_sum(gram(current, current), F32)
    sent = jnp.broadcast_to(own_rows[None], (2 * VOX,) + own_rows.shape)
    aa = lax.all_to_all(sent, ("grp", "vox"), 0, 0, axis_index_groups=shared_groups(1))
    aa = aa.reshape(2, N, N)
    cross = collect(scatter_sum(gram(current, other), F32), F32)
    current = merge(sec, aa, cross, current, other)
    for mask in (2, 4):
        other = partner(current, mask)
        cross = collect(scatter_sum(gram(current, other), BF16), BF16)
        current = merge(sec, None, cross, current, other)
    loadings = scatter_sum(gram(current, series), BF16)
    return loadings[None]


def solution(mesh):
    return jax.shard_map(
        local,
        mesh=mesh,
        in_specs=(P("grp", "vox", None), P("grp", "vox", None)),
        out_specs=P("grp", "vox", None),
        check_vma=False,
    )
```

```python
import functools

import jax
import jax.numpy as jnp
from jax import lax
from jax.experimental import pallas as pl
from jax.experimental.pallas import tpu as pltpu
from jax.sharding import PartitionSpec as P

N = 256
VOX = 16
GRP = 32
ROWS = N // VOX
F32 = jnp.float32
BF16 = jnp.bfloat16

NN = (((1,), (0,)), ((), ()))
NT = (((1,), (1,)), ((), ()))
TN = (((0,), (0,)), ((), ()))
VMEM = pl.BlockSpec(memory_space=pltpu.VMEM)
SMEM = pl.BlockSpec(memory_space=pltpu.SMEM)
PARAMS = pltpu.CompilerParams(vmem_limit_bytes=48 << 20)


def dot1(a, b, dims):
    return lax.dot_general(a.astype(BF16), b.astype(BF16), dims, preferred_element_type=F32)


def split(x):
    hi = x.astype(BF16)
    return hi, (x - hi.astype(F32)).astype(BF16)


def dot3(a, b, dims):
    dot = functools.partial(lax.dot_general, dimension_numbers=dims, preferred_element_type=F32)
    return dot(a[0], b[0]) + (dot(a[0], b[1]) + dot(a[1], b[0]))


def dot_full(a, b, dims):
    return lax.dot_general(a, b, dims, preferred_element_type=F32, precision=lax.Precision.HIGHEST)


def iotas():
    shape = (N, N)
    return lax.broadcasted_iota(jnp.int32, shape, 0), lax.broadcasted_iota(jnp.int32, shape, 1)


def inv_sqrt_diag(m, eye):
    picked = jnp.where(eye, m, 0.0)
    col = lax.rsqrt(jnp.sum(picked, axis=1, keepdims=True))
    row = lax.rsqrt(jnp.sum(picked, axis=0, keepdims=True))
    return col, row


def inverse_factor(m):
    r, c = iotas()
    eye = r == c
    below = r > c
    one = jnp.where(eye, 1.0, 0.0)
    col, start = inv_sqrt_diag(m, eye)
    m = col * m * start
    s = jnp.where(below, m, 0.0)
    s2 = dot1(s, s, NN)
    t = one - s
    x = t + dot1(t, s2, NN)
    for _ in range(2):
        mk = dot1(dot1(x, m, NN), x, NT)
        col, row = inv_sqrt_diag(mk, eye)
        s = jnp.where(below, col * mk * row, 0.0)
        s2 = dot1(s, s, NN)
        t = one - s
        x = col * x
        x = x - dot1(s, x, NN) + dot1(dot1(t, s2, NN), x, NN)
    x = jnp.where(r >= c, x, 0.0)
    xs = split(x)
    mk = dot3(split(dot3(xs, split(m), NN)), xs, NT)
    col, row = inv_sqrt_diag(mk, eye)
    off = jnp.where(eye, 0.0, col * mk * row)
    size = jnp.sum(off * off)
    s = jnp.where(below, off, 0.0)
    x = col * x
    step = s - dot1(s, s, NN)
    x = x - dot3(split(step), split(x), NN)
    return x * start, size


def factor_columns(m_ref, l_ref):
    r, c = iotas()

    def body(j, _):
        m = m_ref[...]
        row = jnp.sum(jnp.where(r == j, m, 0.0), axis=0, keepdims=True)
        col = jnp.sum(jnp.where(c == j, m, 0.0), axis=1, keepdims=True)
        pivot = jnp.sum(jnp.where((r == j) & (c == j), m, 0.0))
        pivot = jnp.full((1, N), pivot, F32)
        row = jnp.where(c[:1] >= j, row, 0.0)
        col = jnp.where(r[:, :1] >= j, col, 0.0)
        m_ref[...] = m - col * (row / pivot)
        l_ref[...] = jnp.where(c == j, col / jnp.sqrt(pivot), l_ref[...])
        return 0

    lax.fori_loop(0, N, body, 0)


def invert_lower(l_ref, x_ref):
    r, c = iotas()
    eye = r == c
    diag = jnp.sum(jnp.where(eye, l_ref[...], 0.0), axis=1, keepdims=True)
    x_ref[...] = jnp.where(eye, 1.0 / diag, 0.0)

    def body(k, _):
        rk, ck = r >> k, c >> k
        off = jnp.where(((rk >> 1) == (ck >> 1)) & (rk > ck), l_ref[...], 0.0)
        x = x_ref[...]
        x_ref[...] = x - dot_full(dot_full(x, off, NN), x, NN)
        return 0

    lax.fori_loop(0, 8, body, 0)


def weights_body(a, b, cross, out_ref, y_ref, z_ref, m_ref, l_ref):
    plain = a is None
    r, c = iotas()
    if plain:
        one = jnp.where(r == c, 1.0, 0.0)
        t0, t1 = one + cross.T, one + cross
        unscale = 1.0
    else:
        top = jnp.max(jnp.where(r == c, jnp.maximum(a, b), 0.0))
        top = jnp.full((1, N), top, F32)
        inv = 1.0 / top
        unscale = lax.rsqrt(top)
        a, b, cross = a * inv, b * inv, cross * inv
        sa, sb = split(a), split(b)
        t0, t1 = a + cross.T, b + cross
    sc = split(cross)

    def times(t0, t1):
        s0, s1 = split(t0), split(t1)
        left, right = dot3(s1, sc, NT), dot3(s0, sc, NN)
        if plain:
            return t0 + left, t1 + right
        return dot3(s0, sa, NN) + left, dot3(s1, sb, NN) + right

    u0, u1 = times(t0, t1)
    v0, v1 = times(u0, u1)
    us0, us1 = split(u0), split(u1)
    m = dot3(split(v0), us0, NT) + dot3(split(v1), us1, NT)
    x, size = inverse_factor(m)
    xs = split(x)
    out_ref[0] = (dot3(xs, us0, NN) * unscale).astype(BF16)
    out_ref[1] = (dot3(xs, us1, NN) * unscale).astype(BF16)
    good = jnp.where(size < 0.01, 1, 0)

    @pl.when(good == 0)
    def _():
        y_ref[0] = t0
        y_ref[1] = t1

        def step(it, _):
            y0, y1 = y_ref[0], y_ref[1]
            left, right = dot_full(y1, cross, NT), dot_full(y0, cross, NN)
            if plain:
                z0, z1 = y0 + left, y1 + right
            else:
                z0, z1 = dot_full(y0, a, NN) + left, dot_full(y1, b, NN) + right
            m_ref[...] = dot_full(z0, y0, NT) + dot_full(z1, y1, NT)
            z_ref[0] = jnp.where(it == 0, z0, y0)
            z_ref[1] = jnp.where(it == 0, z1, y1)
            l_ref[...] = jnp.zeros((N, N), F32)
            factor_columns(m_ref, l_ref)
            invert_lower(l_ref, m_ref)
            xi = m_ref[...]
            y_ref[0] = dot_full(xi, z_ref[0], NN)
            y_ref[1] = dot_full(xi, z_ref[1], NN)
            return 0

        lax.fori_loop(0, 2, step, 0)
        out_ref[0] = (y_ref[0] * unscale).astype(BF16)
        out_ref[1] = (y_ref[1] * unscale).astype(BF16)


SCRATCH = [pltpu.VMEM((2, N, N), F32)] * 2 + [pltpu.VMEM((N, N), F32)] * 2
WEIGHTS = jax.ShapeDtypeStruct((2, N, N), BF16)


def full_kernel(core_ref, mine_ref, theirs_ref, out_ref, g_ref, *scratch):
    core = core_ref[0]
    for y in range(8):
        for k in range(3):
            at = pl.multiple_of(2 * ROWS * y + ROWS * core, ROWS)
            g_ref[k, pl.ds(at, ROWS), :] = mine_ref[y, ROWS * k : ROWS * (k + 1), :]
            at = pl.multiple_of(2 * ROWS * y + ROWS * (1 - core), ROWS)
            g_ref[k, pl.ds(at, ROWS), :] = theirs_ref[y, ROWS * k : ROWS * (k + 1), :]
    weights_body(g_ref[0], g_ref[1], g_ref[2], out_ref, *scratch)


def full_weights(core, mine, theirs):
    return pl.pallas_call(
        full_kernel,
        out_shape=WEIGHTS,
        in_specs=[SMEM, VMEM, VMEM],
        out_specs=VMEM,
        scratch_shapes=[pltpu.VMEM((3, N, N), F32)] + SCRATCH,
        compiler_params=PARAMS,
        name="full_weights",
    )(core, mine, theirs)


def plain_kernel(cross_ref, out_ref, *scratch):
    weights_body(None, None, cross_ref[...].astype(F32), out_ref, *scratch)


def plain_weights(cross):
    return pl.pallas_call(
        plain_kernel,
        out_shape=WEIGHTS,
        in_specs=[VMEM],
        out_specs=VMEM,
        scratch_shapes=SCRATCH,
        compiler_params=PARAMS,
        name="plain_weights",
    )(cross)


def mix_kernel(p_ref, q_ref, w_ref, out_ref):
    out = dot1(p_ref[...], w_ref[0], NT) + dot1(q_ref[...], w_ref[1], NT)
    out_ref[...] = out.astype(BF16)


def mix(p, q, w):
    return pl.pallas_call(
        mix_kernel,
        out_shape=jax.ShapeDtypeStruct(p.shape, BF16),
        in_specs=[VMEM] * 3,
        out_specs=VMEM,
        compiler_params=PARAMS,
        name="mix",
    )(p, q, w)


def mix_cross_kernel(p_ref, q_ref, w_ref, left_ref, out_ref, cross_ref):
    out = dot1(p_ref[...], w_ref[0], NT) + dot1(q_ref[...], w_ref[1], NT)
    out = out.astype(BF16)
    out_ref[...] = out
    cross_ref[...] = dot1(left_ref[...], out, TN).astype(BF16)


def mix_cross(p, q, w, left):
    return pl.pallas_call(
        mix_cross_kernel,
        out_shape=(jax.ShapeDtypeStruct(p.shape, BF16), jax.ShapeDtypeStruct((N, N), BF16)),
        in_specs=[VMEM] * 4,
        out_specs=(VMEM, VMEM),
        compiler_params=PARAMS,
        name="mix_cross",
    )(p, q, w, left)


def gram(a, b):
    return lax.dot_general(a, b, TN, preferred_element_type=F32)


def partner(value, mask):
    return lax.ppermute(value, "grp", [(g, g ^ mask) for g in range(GRP)])


def scatter_sum(value):
    parts = value.reshape((VOX, value.shape[0] // VOX) + value.shape[1:])
    parts = lax.all_to_all(parts, "vox", 0, 0)
    return jnp.sum(parts.astype(F32), axis=0)


def collect(rows):
    sent = jnp.broadcast_to(rows[None], (VOX,) + rows.shape)
    return lax.all_to_all(sent, "vox", 0, 0).reshape((-1,) + rows.shape[1:])


def collect_halves(rows):
    same_core = [[2 * y + c for y in range(8)] for c in range(2)]
    sent = jnp.broadcast_to(rows[None], (8,) + rows.shape)
    mine = lax.all_to_all(sent, "vox", 0, 0, axis_index_groups=same_core)
    return mine, lax.ppermute(mine, "vox", [(v, v ^ 1) for v in range(VOX)])


def local(group_basis, timeseries):
    own = group_basis[0]
    series = timeseries[0]
    core = (lax.axis_index("vox") & 1).astype(jnp.int32).reshape(1)
    other = partner(own, 1)
    own_rows = scatter_sum(gram(own, own))
    own_late, other_late = lax.optimization_barrier((own, other))
    far_own = partner(own_late, 2)
    far_other = partner(other_late, 2)
    other_rows = partner(own_rows, 1)
    cross_rows = scatter_sum(gram(own, other))
    mine, theirs = collect_halves(jnp.concatenate([own_rows, other_rows, cross_rows], axis=0))
    w = full_weights(core, mine, theirs)
    far_w = partner(w, 2)
    node = mix(own, other, w)
    far, cross = mix_cross(far_own, far_other, far_w, node)
    cross = collect(scatter_sum(cross).astype(BF16))
    node = mix(node, far, plain_weights(cross))
    far = partner(node, 4)
    cross = collect(scatter_sum(gram(node, far).astype(BF16)).astype(BF16))
    node = mix(node, far, plain_weights(cross))
    loadings = scatter_sum(gram(node, series).astype(BF16))
    return loadings[None]


def solution(mesh):
    return jax.shard_map(
        local,
        mesh=mesh,
        in_specs=(P("grp", "vox", None), P("grp", "vox", None)),
        out_specs=P("grp", "vox", None),
        check_vma=False,
    )
```

```python
import functools

import jax
import jax.numpy as jnp
from jax import lax
from jax.experimental import pallas as pl
from jax.experimental.pallas import tpu as pltpu
from jax.sharding import PartitionSpec as P


N = 256
VOX = 16
GRP = 32
ROWS = N // VOX
F32 = jnp.float32
BF16 = jnp.bfloat16

NN = (((1,), (0,)), ((), ()))
NT = (((1,), (1,)), ((), ()))
TN = (((0,), (0,)), ((), ()))
VMEM = pl.BlockSpec(memory_space=pltpu.VMEM)
SMEM = pl.BlockSpec(memory_space=pltpu.SMEM)
PARAMS = pltpu.CompilerParams(vmem_limit_bytes=48 << 20)


def dot1(a, b, dims):
    return lax.dot_general(a.astype(BF16), b.astype(BF16), dims, preferred_element_type=F32)


def split(x):
    hi = x.astype(BF16)
    return hi, (x - hi.astype(F32)).astype(BF16)


def dot3(a, b, dims):
    dot = functools.partial(lax.dot_general, dimension_numbers=dims, preferred_element_type=F32)
    return dot(a[0], b[0]) + (dot(a[0], b[1]) + dot(a[1], b[0]))


def dot_full(a, b, dims):
    return lax.dot_general(a, b, dims, preferred_element_type=F32, precision=lax.Precision.HIGHEST)


def iotas():
    shape = (N, N)
    return lax.broadcasted_iota(jnp.int32, shape, 0), lax.broadcasted_iota(jnp.int32, shape, 1)


def inv_sqrt_diag(m, eye):
    picked = jnp.where(eye, m, 0.0)
    col = lax.rsqrt(jnp.sum(picked, axis=1, keepdims=True))
    row = lax.rsqrt(jnp.sum(picked, axis=0, keepdims=True))
    return col, row


def inverse_factor(m):
    r, c = iotas()
    eye = r == c
    below = r > c
    one = jnp.where(eye, 1.0, 0.0)
    col, start = inv_sqrt_diag(m, eye)
    m = col * m * start
    s = jnp.where(below, m, 0.0)
    s2 = dot1(s, s, NN)
    t = one - s
    x = t + dot1(t, s2, NN)
    for _ in range(2):
        mk = dot1(dot1(x, m, NN), x, NT)
        col, row = inv_sqrt_diag(mk, eye)
        s = jnp.where(below, col * mk * row, 0.0)
        s2 = dot1(s, s, NN)
        t = one - s
        x = col * x
        x = x - dot1(s, x, NN) + dot1(dot1(t, s2, NN), x, NN)
    x = jnp.where(r >= c, x, 0.0)
    xs = split(x)
    mk = dot3(split(dot3(xs, split(m), NN)), xs, NT)
    col, row = inv_sqrt_diag(mk, eye)
    off = jnp.where(eye, 0.0, col * mk * row)
    size = jnp.sum(off * off)
    s = jnp.where(below, off, 0.0)
    x = col * x
    step = s - dot1(s, s, NN)
    x = x - dot3(split(step), split(x), NN)
    return x * start, size


def factor_columns(m_ref, l_ref):
    r, c = iotas()

    def body(j, _):
        m = m_ref[...]
        row = jnp.sum(jnp.where(r == j, m, 0.0), axis=0, keepdims=True)
        col = jnp.sum(jnp.where(c == j, m, 0.0), axis=1, keepdims=True)
        pivot = jnp.sum(jnp.where((r == j) & (c == j), m, 0.0))
        pivot = jnp.full((1, N), pivot, F32)
        row = jnp.where(c[:1] >= j, row, 0.0)
        col = jnp.where(r[:, :1] >= j, col, 0.0)
        m_ref[...] = m - col * (row / pivot)
        l_ref[...] = jnp.where(c == j, col / jnp.sqrt(pivot), l_ref[...])
        return 0

    lax.fori_loop(0, N, body, 0)


def invert_lower(l_ref, x_ref):
    r, c = iotas()
    eye = r == c
    diag = jnp.sum(jnp.where(eye, l_ref[...], 0.0), axis=1, keepdims=True)
    x_ref[...] = jnp.where(eye, 1.0 / diag, 0.0)

    def body(k, _):
        rk, ck = r >> k, c >> k
        off = jnp.where(((rk >> 1) == (ck >> 1)) & (rk > ck), l_ref[...], 0.0)
        x = x_ref[...]
        x_ref[...] = x - dot_full(dot_full(x, off, NN), x, NN)
        return 0

    lax.fori_loop(0, 8, body, 0)


def weights_body(a, b, cross, out_ref, y_ref, z_ref, m_ref, l_ref):
    plain = a is None
    r, c = iotas()
    if plain:
        one = jnp.where(r == c, 1.0, 0.0)
        t0, t1 = one + cross.T, one + cross
        unscale = 1.0
    else:
        top = jnp.max(jnp.where(r == c, jnp.maximum(a, b), 0.0))
        top = jnp.full((1, N), top, F32)
        inv = 1.0 / top
        unscale = lax.rsqrt(top)
        a, b, cross = a * inv, b * inv, cross * inv
        sa, sb = split(a), split(b)
        t0, t1 = a + cross.T, b + cross
    sc = split(cross)

    def times(t0, t1):
        s0, s1 = split(t0), split(t1)
        left, right = dot3(s1, sc, NT), dot3(s0, sc, NN)
        if plain:
            return t0 + left, t1 + right
        return dot3(s0, sa, NN) + left, dot3(s1, sb, NN) + right

    u0, u1 = times(t0, t1)
    v0, v1 = times(u0, u1)
    us0, us1 = split(u0), split(u1)
    m = dot3(split(v0), us0, NT) + dot3(split(v1), us1, NT)
    x, size = inverse_factor(m)
    xs = split(x)
    out_ref[0] = (dot3(xs, us0, NN) * unscale).astype(BF16)
    out_ref[1] = (dot3(xs, us1, NN) * unscale).astype(BF16)
    good = jnp.where(size < 0.01, 1, 0)

    @pl.when(good == 0)
    def _():
        y_ref[0] = t0
        y_ref[1] = t1

        def step(it, _):
            y0, y1 = y_ref[0], y_ref[1]
            left, right = dot_full(y1, cross, NT), dot_full(y0, cross, NN)
            if plain:
                z0, z1 = y0 + left, y1 + right
            else:
                z0, z1 = dot_full(y0, a, NN) + left, dot_full(y1, b, NN) + right
            m_ref[...] = dot_full(z0, y0, NT) + dot_full(z1, y1, NT)
            z_ref[0] = jnp.where(it == 0, z0, y0)
            z_ref[1] = jnp.where(it == 0, z1, y1)
            l_ref[...] = jnp.zeros((N, N), F32)
            factor_columns(m_ref, l_ref)
            invert_lower(l_ref, m_ref)
            xi = m_ref[...]
            y_ref[0] = dot_full(xi, z_ref[0], NN)
            y_ref[1] = dot_full(xi, z_ref[1], NN)
            return 0

        lax.fori_loop(0, 2, step, 0)
        out_ref[0] = (y_ref[0] * unscale).astype(BF16)
        out_ref[1] = (y_ref[1] * unscale).astype(BF16)


SCRATCH = [pltpu.VMEM((2, N, N), F32)] * 2 + [pltpu.VMEM((N, N), F32)] * 2
WEIGHTS = jax.ShapeDtypeStruct((2, N, N), BF16)


def full_kernel(core_ref, mine_ref, theirs_ref, out_ref, g_ref, *scratch):
    core = core_ref[0]
    for y in range(8):
        for k in range(3):
            at = pl.multiple_of(2 * ROWS * y + ROWS * core, ROWS)
            g_ref[k, pl.ds(at, ROWS), :] = mine_ref[y, ROWS * k : ROWS * (k + 1), :]
            at = pl.multiple_of(2 * ROWS * y + ROWS * (1 - core), ROWS)
            g_ref[k, pl.ds(at, ROWS), :] = theirs_ref[y, ROWS * k : ROWS * (k + 1), :]
    weights_body(g_ref[0], g_ref[1], g_ref[2], out_ref, *scratch)


def full_weights(core, mine, theirs):
    return pl.pallas_call(
        full_kernel,
        out_shape=WEIGHTS,
        in_specs=[SMEM, VMEM, VMEM],
        out_specs=VMEM,
        scratch_shapes=[pltpu.VMEM((3, N, N), F32)] + SCRATCH,
        compiler_params=PARAMS,
        name="full_weights",
    )(core, mine, theirs)


def plain_kernel(cross_ref, out_ref, *scratch):
    weights_body(None, None, cross_ref[...].astype(F32), out_ref, *scratch)


def plain_weights(cross):
    return pl.pallas_call(
        plain_kernel,
        out_shape=WEIGHTS,
        in_specs=[VMEM],
        out_specs=VMEM,
        scratch_shapes=SCRATCH,
        compiler_params=PARAMS,
        name="plain_weights",
    )(cross)


def mix_kernel(p_ref, q_ref, w_ref, out_ref):
    out = dot1(p_ref[...], w_ref[0], NT) + dot1(q_ref[...], w_ref[1], NT)
    out_ref[...] = out.astype(BF16)


def mix(p, q, w):
    return pl.pallas_call(
        mix_kernel,
        out_shape=jax.ShapeDtypeStruct(p.shape, BF16),
        in_specs=[VMEM] * 3,
        out_specs=VMEM,
        compiler_params=PARAMS,
        name="mix",
    )(p, q, w)


def mix_cross_kernel(p_ref, q_ref, w_ref, left_ref, out_ref, cross_ref):
    out = dot1(p_ref[...], w_ref[0], NT) + dot1(q_ref[...], w_ref[1], NT)
    out = out.astype(BF16)
    out_ref[...] = out
    cross_ref[...] = dot1(left_ref[...], out, TN).astype(BF16)


def mix_cross(p, q, w, left):
    return pl.pallas_call(
        mix_cross_kernel,
        out_shape=(jax.ShapeDtypeStruct(p.shape, BF16), jax.ShapeDtypeStruct((N, N), BF16)),
        in_specs=[VMEM] * 4,
        out_specs=(VMEM, VMEM),
        compiler_params=PARAMS,
        name="mix_cross",
    )(p, q, w, left)


def gram(a, b):
    return lax.dot_general(a, b, TN, preferred_element_type=F32)


def partner(value, mask):
    return lax.ppermute(value, "grp", [(g, g ^ mask) for g in range(GRP)])


def scatter_sum(value):
    parts = value.reshape((VOX, value.shape[0] // VOX) + value.shape[1:])
    parts = lax.all_to_all(parts, "vox", 0, 0)
    return jnp.sum(parts.astype(F32), axis=0)


def collect(rows):
    sent = jnp.broadcast_to(rows[None], (VOX,) + rows.shape)
    return lax.all_to_all(sent, "vox", 0, 0).reshape((-1,) + rows.shape[1:])


def collect_halves(rows):
    same_core = [[2 * y + c for y in range(8)] for c in range(2)]
    sent = jnp.broadcast_to(rows[None], (8,) + rows.shape)
    mine = lax.all_to_all(sent, "vox", 0, 0, axis_index_groups=same_core)
    return mine, lax.ppermute(mine, "vox", [(v, v ^ 1) for v in range(VOX)])


def tree(own, series):
    core = (lax.axis_index("vox") & 1).astype(jnp.int32).reshape(1)
    other = partner(own, 1)
    own_rows = scatter_sum(gram(own, own))
    own_late, other_late = lax.optimization_barrier((own, other))
    far_own = partner(own_late, 2)
    far_other = partner(other_late, 2)
    other_rows = partner(own_rows, 1)
    cross_rows = scatter_sum(gram(own, other))
    rows = jnp.concatenate([own_rows, other_rows, cross_rows], axis=0)
    mine, theirs = collect_halves(rows)
    w = full_weights(core, mine, theirs)
    far_w = partner(w, 2)
    left = mix(own, other, w)
    deep_left = partner(left, 4)
    right, cross = mix_cross(far_own, far_other, far_w, left)
    deep_right = partner(right, 4)
    rows = scatter_sum(cross)
    cross = collect(rows.astype(BF16))
    w = plain_weights(cross)
    deep_w = partner(w, 4)
    left = mix(left, right, w)
    right, cross = mix_cross(deep_left, deep_right, deep_w, left)
    rows = scatter_sum(cross)
    cross = collect(rows.astype(BF16))
    root = mix(left, right, plain_weights(cross))
    return scatter_sum(gram(root, series).astype(BF16))


def local(group_basis, timeseries):
    return tree(group_basis[0], timeseries[0])[None]


def solution(mesh):
    return jax.shard_map(
        local,
        mesh=mesh,
        in_specs=(P("grp", "vox", None), P("grp", "vox", None)),
        out_specs=P("grp", "vox", None),
        check_vma=False,
    )
```

```python
import functools

import jax
import jax.numpy as jnp
from jax import lax
from jax.experimental import pallas as pl
from jax.experimental.pallas import tpu as pltpu
from jax.sharding import PartitionSpec as P


N = 256
H = 128
VOX = 16
GRP = 32
ROWS = N // VOX
F32 = jnp.float32
BF16 = jnp.bfloat16

NN = (((1,), (0,)), ((), ()))
NT = (((1,), (1,)), ((), ()))
TN = (((0,), (0,)), ((), ()))
VMEM = pl.BlockSpec(memory_space=pltpu.VMEM)
SMEM = pl.BlockSpec(memory_space=pltpu.SMEM)
PARAMS = pltpu.CompilerParams(vmem_limit_bytes=16 << 20)


def dot1(a, b, dims):
    return lax.dot_general(a.astype(BF16), b.astype(BF16), dims, preferred_element_type=F32)


def split(x):
    hi = x.astype(BF16)
    return hi, (x - hi.astype(F32)).astype(BF16)


def dot3(a, b, dims):
    dot = functools.partial(lax.dot_general, dimension_numbers=dims, preferred_element_type=F32)
    return dot(a[0], b[0]) + (dot(a[0], b[1]) + dot(a[1], b[0]))


def dot_full(a, b, dims):
    return lax.dot_general(a, b, dims, preferred_element_type=F32, precision=lax.Precision.HIGHEST)


def iotas():
    shape = (N, N)
    return lax.broadcasted_iota(jnp.int32, shape, 0), lax.broadcasted_iota(jnp.int32, shape, 1)


def inv_sqrt_diag(m, eye):
    picked = jnp.where(eye, m, 0.0)
    col = lax.rsqrt(jnp.sum(picked, axis=1, keepdims=True))
    row = lax.rsqrt(jnp.sum(picked, axis=0, keepdims=True))
    return col, row


def inverse_factor(m):
    r, c = iotas()
    eye = r == c
    below = r > c
    one = jnp.where(eye, 1.0, 0.0)
    col, start = inv_sqrt_diag(m, eye)
    m = col * m * start
    s = jnp.where(below, m, 0.0)
    s2 = dot1(s, s, NN)
    t = one - s
    x = t + dot1(t, s2, NN)
    for _ in range(2):
        mk = dot1(dot1(x, m, NN), x, NT)
        col, row = inv_sqrt_diag(mk, eye)
        s = jnp.where(below, col * mk * row, 0.0)
        s2 = dot1(s, s, NN)
        t = one - s
        x = col * x
        x = x - dot1(s, x, NN) + dot1(dot1(t, s2, NN), x, NN)
    x = jnp.where(r >= c, x, 0.0)
    xs = split(x)
    mk = dot3(split(dot3(xs, split(m), NN)), xs, NT)
    col, row = inv_sqrt_diag(mk, eye)
    off = jnp.where(eye, 0.0, col * mk * row)
    size = jnp.sum(off * off)
    s = jnp.where(below, off, 0.0)
    x = col * x
    step = s - dot1(s, s, NN)
    x = x - dot3(split(step), split(x), NN)
    return x * start, size


def factor_columns(m_ref, l_ref):
    r, c = iotas()

    def body(j, _):
        m = m_ref[...]
        row = jnp.sum(jnp.where(r == j, m, 0.0), axis=0, keepdims=True)
        col = jnp.sum(jnp.where(c == j, m, 0.0), axis=1, keepdims=True)
        pivot = jnp.sum(jnp.where((r == j) & (c == j), m, 0.0))
        pivot = jnp.full((1, N), pivot, F32)
        row = jnp.where(c[:1] >= j, row, 0.0)
        col = jnp.where(r[:, :1] >= j, col, 0.0)
        m_ref[...] = m - col * (row / pivot)
        l_ref[...] = jnp.where(c == j, col / jnp.sqrt(pivot), l_ref[...])
        return 0

    lax.fori_loop(0, N, body, 0)


def invert_lower(l_ref, x_ref):
    r, c = iotas()
    eye = r == c
    diag = jnp.sum(jnp.where(eye, l_ref[...], 0.0), axis=1, keepdims=True)
    x_ref[...] = jnp.where(eye, 1.0 / diag, 0.0)

    def body(k, _):
        rk, ck = r >> k, c >> k
        off = jnp.where(((rk >> 1) == (ck >> 1)) & (rk > ck), l_ref[...], 0.0)
        x = x_ref[...]
        x_ref[...] = x - dot_full(dot_full(x, off, NN), x, NN)
        return 0

    lax.fori_loop(0, 8, body, 0)


def weights_body(a, b, cross, out_ref, y_ref, z_ref, m_ref, l_ref):
    plain = a is None
    r, c = iotas()
    if plain:
        one = jnp.where(r == c, 1.0, 0.0)
        t0, t1 = one + cross.T, one + cross
        unscale = 1.0
    else:
        top = jnp.max(jnp.where(r == c, jnp.maximum(a, b), 0.0))
        top = jnp.full((1, N), top, F32)
        inv = 1.0 / top
        unscale = lax.rsqrt(top)
        a, b, cross = a * inv, b * inv, cross * inv
        sa, sb = split(a), split(b)
        t0, t1 = a + cross.T, b + cross
    sc = split(cross)

    def times(t0, t1):
        s0, s1 = split(t0), split(t1)
        left, right = dot3(s1, sc, NT), dot3(s0, sc, NN)
        if plain:
            return t0 + left, t1 + right
        return dot3(s0, sa, NN) + left, dot3(s1, sb, NN) + right

    u0, u1 = times(t0, t1)
    v0, v1 = times(u0, u1)
    us0, us1 = split(u0), split(u1)
    m = dot3(split(v0), us0, NT) + dot3(split(v1), us1, NT)
    x, size = inverse_factor(m)
    xs = split(x)
    out_ref[0] = (dot3(xs, us0, NN) * unscale).astype(BF16)
    out_ref[1] = (dot3(xs, us1, NN) * unscale).astype(BF16)
    good = jnp.where(size < 0.01, 1, 0)

    @pl.when(good == 0)
    def _():
        y_ref[0] = t0
        y_ref[1] = t1

        def step(it, _):
            y0, y1 = y_ref[0], y_ref[1]
            left, right = dot_full(y1, cross, NT), dot_full(y0, cross, NN)
            if plain:
                z0, z1 = y0 + left, y1 + right
            else:
                z0, z1 = dot_full(y0, a, NN) + left, dot_full(y1, b, NN) + right
            m_ref[...] = dot_full(z0, y0, NT) + dot_full(z1, y1, NT)
            z_ref[0] = jnp.where(it == 0, z0, y0)
            z_ref[1] = jnp.where(it == 0, z1, y1)
            l_ref[...] = jnp.zeros((N, N), F32)
            factor_columns(m_ref, l_ref)
            invert_lower(l_ref, m_ref)
            xi = m_ref[...]
            y_ref[0] = dot_full(xi, z_ref[0], NN)
            y_ref[1] = dot_full(xi, z_ref[1], NN)
            return 0

        lax.fori_loop(0, 2, step, 0)
        out_ref[0] = (y_ref[0] * unscale).astype(BF16)
        out_ref[1] = (y_ref[1] * unscale).astype(BF16)


SCRATCH = [pltpu.VMEM((2, N, N), F32)] * 2 + [pltpu.VMEM((N, N), F32)] * 2
WEIGHTS = jax.ShapeDtypeStruct((2, N, N), BF16)


def full_kernel(core_ref, mine_ref, theirs_ref, out_ref, a_ref, c_ref, *scratch):
    core = core_ref[0]
    for half, ref in ((core, mine_ref), (1 - core, theirs_ref)):
        for y in range(8):
            block = 2 * y + half
            lo = pl.ds(pl.multiple_of(8 * block, 8), 8)
            hi = pl.ds(pl.multiple_of(H + 8 * block, 8), 8)
            for k in range(2):
                a_ref[k, lo, :H] = ref[y, 24 * k : 24 * k + 8, :]
                a_ref[k, hi, H:] = ref[y, 24 * k + 8 : 24 * k + 16, :]
                a_ref[k, hi, :H] = ref[y, 24 * k + 16 : 24 * k + 24, :]
            at = pl.ds(pl.multiple_of(ROWS * block, ROWS), ROWS)
            c_ref[at, :H] = ref[y, 48:64, :]
            c_ref[at, H:] = ref[y, 64:80, :]
    for k in range(2):
        a_ref[k, :H, H:] = a_ref[k, H:, :H].T
    weights_body(a_ref[0], a_ref[1], c_ref[...], out_ref, *scratch)


def full_weights(core, mine, theirs):
    return pl.pallas_call(
        full_kernel,
        out_shape=WEIGHTS,
        in_specs=[SMEM, VMEM, VMEM],
        out_specs=VMEM,
        scratch_shapes=[pltpu.VMEM((2, N, N), F32), pltpu.VMEM((N, N), F32)] + SCRATCH,
        compiler_params=PARAMS,
        name="full_weights",
    )(core, mine, theirs)


def plain_kernel(cross_ref, out_ref, *scratch):
    weights_body(None, None, cross_ref[...].astype(F32), out_ref, *scratch)


def plain_weights(cross):
    return pl.pallas_call(
        plain_kernel,
        out_shape=WEIGHTS,
        in_specs=[VMEM],
        out_specs=VMEM,
        scratch_shapes=SCRATCH,
        compiler_params=PARAMS,
        name="plain_weights",
    )(cross)


def mix_kernel(p_ref, q_ref, w_ref, out_ref):
    out = dot1(p_ref[...], w_ref[0], NT) + dot1(q_ref[...], w_ref[1], NT)
    out_ref[...] = out.astype(BF16)


def mix(p, q, w):
    return pl.pallas_call(
        mix_kernel,
        out_shape=jax.ShapeDtypeStruct(p.shape, BF16),
        in_specs=[VMEM] * 3,
        out_specs=VMEM,
        compiler_params=PARAMS,
        name="mix",
    )(p, q, w)


def project_kernel(p_ref, q_ref, w_ref, *refs):
    sides, (out_ref, proj_ref) = refs[:-2], refs[-2:]
    out = dot1(p_ref[...], w_ref[0], NT) + dot1(q_ref[...], w_ref[1], NT)
    out = out.astype(BF16)
    out_ref[...] = out
    at = 0
    for side in sides:
        width = side.shape[1]
        got = dot1(out, side[...], TN).astype(BF16)
        proj_ref[:, :, at : at + width] = got.reshape(VOX, ROWS, width)
        at += width


def project(p, q, w, *sides):
    width = sum(side.shape[1] for side in sides)
    return pl.pallas_call(
        project_kernel,
        out_shape=(
            jax.ShapeDtypeStruct(p.shape, BF16),
            jax.ShapeDtypeStruct((VOX, ROWS, width), BF16),
        ),
        in_specs=[VMEM] * (3 + len(sides)),
        out_specs=(VMEM, VMEM),
        compiler_params=PARAMS,
        name="project",
    )(p, q, w, *sides)


def self_gram_kernel(p_ref, out_ref):
    left, right = p_ref[:, :H], p_ref[:, H:]
    for k, (a, b) in enumerate(((left, left), (right, right), (right, left))):
        out_ref[:, 8 * k : 8 * k + 8, :] = dot1(a, b, TN).reshape(VOX, 8, H)


def self_gram(p):
    return pl.pallas_call(
        self_gram_kernel,
        out_shape=jax.ShapeDtypeStruct((VOX, 24, H), F32),
        in_specs=[VMEM],
        out_specs=VMEM,
        compiler_params=PARAMS,
        name="self_gram",
    )(p)


def cross_gram_kernel(p_ref, q_ref, out_ref):
    got = dot1(p_ref[...], q_ref[...], TN)
    out_ref[:, :ROWS, :] = got[:, :H].reshape(VOX, ROWS, H)
    out_ref[:, ROWS:, :] = got[:, H:].reshape(VOX, ROWS, H)


def cross_gram(p, q):
    return pl.pallas_call(
        cross_gram_kernel,
        out_shape=jax.ShapeDtypeStruct((VOX, 2 * ROWS, H), F32),
        in_specs=[VMEM, VMEM],
        out_specs=VMEM,
        compiler_params=PARAMS,
        name="cross_gram",
    )(p, q)


def rows_kernel(parts_ref, w_ref, out_ref):
    total = jnp.sum(parts_ref[...].astype(F32), axis=0)
    hi, lo = split(total)
    got = jnp.zeros((ROWS, N), F32)
    for k in range(2):
        at = slice(N * k, N * (k + 1))
        got = got + (dot1(hi[:, at], w_ref[k], NT) + dot1(lo[:, at], w_ref[k], NT))
    out_ref[...] = jnp.broadcast_to(got.astype(BF16)[None], out_ref.shape)


def cross_rows_of(parts, w):
    return pl.pallas_call(
        rows_kernel,
        out_shape=jax.ShapeDtypeStruct((VOX, ROWS, N), BF16),
        in_specs=[VMEM, VMEM],
        out_specs=VMEM,
        compiler_params=PARAMS,
        name="cross_rows",
    )(parts, w)


def partner(value, mask):
    return lax.ppermute(value, "grp", [(g, g ^ mask) for g in range(GRP)])


def exchange(parts):
    return lax.all_to_all(parts, "vox", 0, 0)


def same_core(rows):
    groups = [[2 * y + c for y in range(8)] for c in range(2)]
    sent = jnp.broadcast_to(rows[None], (8,) + rows.shape)
    return lax.all_to_all(sent, "vox", 0, 0, axis_index_groups=groups)


def swap_cores(value):
    return lax.ppermute(value, "vox", [(v, v ^ 1) for v in range(VOX)])


def add_up(parts):
    return jnp.sum(parts.astype(F32), axis=0)


def tree(own, series):
    core = (lax.axis_index("vox") & 1).astype(jnp.int32).reshape(1)
    other = partner(own, 1)
    own_rows = add_up(exchange(self_gram(own)))
    far_own = partner(own, 2)
    far_other = partner(other, 2)
    other_rows = partner(own_rows, 1)
    cross_rows = add_up(exchange(cross_gram(own, other)))
    rows = jnp.concatenate([own_rows, other_rows, cross_rows], axis=0)
    mine = same_core(rows)
    theirs = swap_cores(mine)
    w = full_weights(core, mine, theirs)

    left, parts = project(own, other, w, far_own, far_other)
    parts = exchange(parts)
    far_w = partner(w, 2)
    deep_right = partner(left, 6)
    cross = exchange(cross_rows_of(parts, far_w))
    deep_left = partner(left, 4)
    right = mix(far_own, far_other, far_w)
    w = plain_weights(cross.reshape(N, N))

    left, parts = project(left, right, w, deep_left, deep_right)
    parts = exchange(parts)
    deep_w = partner(w, 4)
    cross = exchange(cross_rows_of(parts, deep_w))
    right = mix(deep_left, deep_right, deep_w)
    w = plain_weights(cross.reshape(N, N))

    _, parts = project(left, right, w, series)
    return add_up(exchange(parts))


def local(group_basis, timeseries):
    return tree(group_basis[0], timeseries[0])[None]


def solution(mesh):
    return jax.shard_map(
        local,
        mesh=mesh,
        in_specs=(P("grp", "vox", None), P("grp", "vox", None)),
        out_specs=P("grp", "vox", None),
        check_vma=False,
    )
```

```python
import functools

import jax
import jax.numpy as jnp
from jax import lax
from jax.experimental import pallas as pl
from jax.experimental.pallas import tpu as pltpu
from jax.sharding import PartitionSpec as P


N = 256
H = 128
VOX = 16
GRP = 32
ROWS = N // VOX
F32 = jnp.float32
BF16 = jnp.bfloat16

NN = (((1,), (0,)), ((), ()))
NT = (((1,), (1,)), ((), ()))
TN = (((0,), (0,)), ((), ()))
VMEM = pl.BlockSpec(memory_space=pltpu.VMEM)
SMEM = pl.BlockSpec(memory_space=pltpu.SMEM)
HBM = pl.BlockSpec(memory_space=pltpu.MemorySpace.HBM)


def params(mib):
    return pltpu.CompilerParams(vmem_limit_bytes=mib << 20)


def dot1(a, b, dims):
    return lax.dot_general(a.astype(BF16), b.astype(BF16), dims, preferred_element_type=F32)


def split(x):
    hi = x.astype(BF16)
    return hi, (x - hi.astype(F32)).astype(BF16)


def dot3(a, b, dims):
    dot = functools.partial(lax.dot_general, dimension_numbers=dims, preferred_element_type=F32)
    return dot(a[0], b[0]) + (dot(a[0], b[1]) + dot(a[1], b[0]))


def dot_full(a, b, dims):
    return lax.dot_general(a, b, dims, preferred_element_type=F32, precision=lax.Precision.HIGHEST)


def iotas():
    shape = (N, N)
    return lax.broadcasted_iota(jnp.int32, shape, 0), lax.broadcasted_iota(jnp.int32, shape, 1)


def inv_sqrt_diag(m, eye):
    picked = jnp.where(eye, m, 0.0)
    col = lax.rsqrt(jnp.sum(picked, axis=1, keepdims=True))
    row = lax.rsqrt(jnp.sum(picked, axis=0, keepdims=True))
    return col, row


def inverse_factor(m):
    r, c = iotas()
    eye = r == c
    below = r > c
    one = jnp.where(eye, 1.0, 0.0)
    col, start = inv_sqrt_diag(m, eye)
    m = col * m * start
    s = jnp.where(below, m, 0.0)
    s2 = dot1(s, s, NN)
    t = one - s
    x = t + dot1(t, s2, NN)
    for _ in range(2):
        mk = dot1(dot1(x, m, NN), x, NT)
        col, row = inv_sqrt_diag(mk, eye)
        s = jnp.where(below, col * mk * row, 0.0)
        s2 = dot1(s, s, NN)
        t = one - s
        x = col * x
        x = x - dot1(s, x, NN) + dot1(dot1(t, s2, NN), x, NN)
    x = jnp.where(r >= c, x, 0.0)
    xs = split(x)
    mk = dot3(split(dot3(xs, split(m), NN)), xs, NT)
    col, row = inv_sqrt_diag(mk, eye)
    off = jnp.where(eye, 0.0, col * mk * row)
    size = jnp.sum(off * off)
    s = jnp.where(below, off, 0.0)
    x = col * x
    step = s - dot1(s, s, NN)
    x = x - dot3(split(step), split(x), NN)
    return x * start, size


def factor_columns(m_ref, l_ref):
    r, c = iotas()

    def body(j, _):
        m = m_ref[...]
        row = jnp.sum(jnp.where(r == j, m, 0.0), axis=0, keepdims=True)
        col = jnp.sum(jnp.where(c == j, m, 0.0), axis=1, keepdims=True)
        pivot = jnp.sum(jnp.where((r == j) & (c == j), m, 0.0))
        pivot = jnp.full((1, N), pivot, F32)
        row = jnp.where(c[:1] >= j, row, 0.0)
        col = jnp.where(r[:, :1] >= j, col, 0.0)
        m_ref[...] = m - col * (row / pivot)
        l_ref[...] = jnp.where(c == j, col / jnp.sqrt(pivot), l_ref[...])
        return 0

    lax.fori_loop(0, N, body, 0)


def invert_lower(l_ref, x_ref):
    r, c = iotas()
    eye = r == c
    diag = jnp.sum(jnp.where(eye, l_ref[...], 0.0), axis=1, keepdims=True)
    x_ref[...] = jnp.where(eye, 1.0 / diag, 0.0)

    def body(k, _):
        rk, ck = r >> k, c >> k
        off = jnp.where(((rk >> 1) == (ck >> 1)) & (rk > ck), l_ref[...], 0.0)
        x = x_ref[...]
        x_ref[...] = x - dot_full(dot_full(x, off, NN), x, NN)
        return 0

    lax.fori_loop(0, 8, body, 0)


def weights_body(a, b, cross, out_ref, y_ref, z_ref, m_ref, l_ref):
    plain = a is None
    r, c = iotas()
    if plain:
        one = jnp.where(r == c, 1.0, 0.0)
        t0, t1 = one + cross.T, one + cross
        unscale = 1.0
    else:
        top = jnp.max(jnp.where(r == c, jnp.maximum(a, b), 0.0))
        top = jnp.full((1, N), top, F32)
        inv = 1.0 / top
        unscale = lax.rsqrt(top)
        a, b, cross = a * inv, b * inv, cross * inv
        sa, sb = split(a), split(b)
        t0, t1 = a + cross.T, b + cross
    sc = split(cross)

    def times(t0, t1):
        s0, s1 = split(t0), split(t1)
        left, right = dot3(s1, sc, NT), dot3(s0, sc, NN)
        if plain:
            return t0 + left, t1 + right
        return dot3(s0, sa, NN) + left, dot3(s1, sb, NN) + right

    u0, u1 = times(t0, t1)
    v0, v1 = times(u0, u1)
    us0, us1 = split(u0), split(u1)
    m = dot3(split(v0), us0, NT) + dot3(split(v1), us1, NT)
    x, size = inverse_factor(m)
    xs = split(x)
    out_ref[0] = (dot3(xs, us0, NN) * unscale).astype(BF16)
    out_ref[1] = (dot3(xs, us1, NN) * unscale).astype(BF16)
    good = jnp.where(size < 0.01, 1, 0)

    @pl.when(good == 0)
    def _():
        y_ref[0] = t0
        y_ref[1] = t1

        def step(it, _):
            y0, y1 = y_ref[0], y_ref[1]
            left, right = dot_full(y1, cross, NT), dot_full(y0, cross, NN)
            if plain:
                z0, z1 = y0 + left, y1 + right
            else:
                z0, z1 = dot_full(y0, a, NN) + left, dot_full(y1, b, NN) + right
            m_ref[...] = dot_full(z0, y0, NT) + dot_full(z1, y1, NT)
            z_ref[0] = jnp.where(it == 0, z0, y0)
            z_ref[1] = jnp.where(it == 0, z1, y1)
            l_ref[...] = jnp.zeros((N, N), F32)
            factor_columns(m_ref, l_ref)
            invert_lower(l_ref, m_ref)
            xi = m_ref[...]
            y_ref[0] = dot_full(xi, z_ref[0], NN)
            y_ref[1] = dot_full(xi, z_ref[1], NN)
            return 0

        lax.fori_loop(0, 2, step, 0)
        out_ref[0] = (y_ref[0] * unscale).astype(BF16)
        out_ref[1] = (y_ref[1] * unscale).astype(BF16)


SCRATCH = [pltpu.VMEM((2, N, N), F32)] * 2 + [pltpu.VMEM((N, N), F32)] * 2
WEIGHTS = jax.ShapeDtypeStruct((2, N, N), BF16)


def full_kernel(core_ref, mine_ref, theirs_ref, out_ref, a_ref, c_ref, *scratch):
    core = core_ref[0]
    for half, ref in ((core, mine_ref), (1 - core, theirs_ref)):
        for y in range(8):
            block = 2 * y + half
            lo = pl.ds(pl.multiple_of(8 * block, 8), 8)
            hi = pl.ds(pl.multiple_of(H + 8 * block, 8), 8)
            for k in range(2):
                a_ref[k, lo, :H] = ref[y, 24 * k : 24 * k + 8, :]
                a_ref[k, hi, H:] = ref[y, 24 * k + 8 : 24 * k + 16, :]
                a_ref[k, hi, :H] = ref[y, 24 * k + 16 : 24 * k + 24, :]
            at = pl.ds(pl.multiple_of(ROWS * block, ROWS), ROWS)
            c_ref[at, :H] = ref[y, 48:64, :]
            c_ref[at, H:] = ref[y, 64:80, :]
    for k in range(2):
        a_ref[k, :H, H:] = a_ref[k, H:, :H].T
    weights_body(a_ref[0], a_ref[1], c_ref[...], out_ref, *scratch)


def full_weights(core, mine, theirs):
    return pl.pallas_call(
        full_kernel,
        out_shape=WEIGHTS,
        in_specs=[SMEM, VMEM, VMEM],
        out_specs=VMEM,
        scratch_shapes=[pltpu.VMEM((2, N, N), F32), pltpu.VMEM((N, N), F32)] + SCRATCH,
        compiler_params=params(12),
        name="full_weights",
    )(core, mine, theirs)


def plain_kernel(cross_ref, out_ref, *scratch):
    weights_body(None, None, cross_ref[...].astype(F32), out_ref, *scratch)


def plain_weights(cross):
    return pl.pallas_call(
        plain_kernel,
        out_shape=WEIGHTS,
        in_specs=[VMEM],
        out_specs=VMEM,
        scratch_shapes=SCRATCH,
        compiler_params=params(12),
        name="plain_weights",
    )(cross)


def mix_kernel(p_ref, q_ref, w_ref, out_ref):
    out = dot1(p_ref[...], w_ref[0], NT) + dot1(q_ref[...], w_ref[1], NT)
    out_ref[...] = out.astype(BF16)


def mix(p, q, w):
    return pl.pallas_call(
        mix_kernel,
        out_shape=jax.ShapeDtypeStruct(p.shape, BF16),
        in_specs=[VMEM] * 3,
        out_specs=VMEM,
        compiler_params=params(6),
        name="mix",
    )(p, q, w)


def project_kernel(p_ref, q_ref, w_ref, r_ref, s_ref, out_hbm, proj_ref, out_ref, sem):
    out = dot1(p_ref[...], w_ref[0], NT) + dot1(q_ref[...], w_ref[1], NT)
    out = out.astype(BF16)
    out_ref[...] = out
    copy = pltpu.make_async_copy(out_ref, out_hbm, sem)
    copy.start()
    for k, side in enumerate((r_ref, s_ref)):
        got = dot1(out, side[...], TN).astype(BF16)
        proj_ref[:, :, N * k : N * (k + 1)] = got.reshape(VOX, ROWS, N)
    copy.wait()


def project(p, q, w, r, s):
    return pl.pallas_call(
        project_kernel,
        out_shape=(
            jax.ShapeDtypeStruct(p.shape, BF16),
            jax.ShapeDtypeStruct((VOX, ROWS, 2 * N), BF16),
        ),
        in_specs=[VMEM] * 5,
        out_specs=(HBM, VMEM),
        scratch_shapes=[pltpu.VMEM(p.shape, BF16), pltpu.SemaphoreType.DMA],
        compiler_params=params(8),
        name="project",
    )(p, q, w, r, s)


def load_kernel(p_hbm, q_ref, w_ref, series_hbm, out_ref, p_ref, series_ref, p_sem, sem):
    first = pltpu.make_async_copy(p_hbm, p_ref, p_sem)
    first.start()
    copy = pltpu.make_async_copy(series_hbm, series_ref, sem)
    copy.start()
    root = dot1(q_ref[...], w_ref[1], NT)
    first.wait()
    root = (root + dot1(p_ref[...], w_ref[0], NT)).astype(BF16)
    copy.wait()
    got = dot1(root, series_ref[...], TN).astype(BF16)
    out_ref[...] = got.reshape(out_ref.shape)


def load(p, q, w, series):
    return pl.pallas_call(
        load_kernel,
        out_shape=jax.ShapeDtypeStruct((VOX, ROWS, series.shape[1]), BF16),
        in_specs=[HBM, VMEM, VMEM, HBM],
        out_specs=VMEM,
        scratch_shapes=[pltpu.VMEM(p.shape, BF16), pltpu.VMEM(series.shape, BF16)]
        + [pltpu.SemaphoreType.DMA] * 2,
        compiler_params=params(8),
        name="load",
    )(p, q, w, series)


def self_gram_kernel(p_ref, out_ref):
    left, right = p_ref[:, :H], p_ref[:, H:]
    for k, (a, b) in enumerate(((left, left), (right, right), (right, left))):
        out_ref[:, 8 * k : 8 * k + 8, :] = dot1(a, b, TN).reshape(VOX, 8, H)


def self_gram(p):
    return pl.pallas_call(
        self_gram_kernel,
        out_shape=jax.ShapeDtypeStruct((VOX, 24, H), F32),
        in_specs=[VMEM],
        out_specs=VMEM,
        compiler_params=params(4),
        name="self_gram",
    )(p)


def cross_gram_kernel(p_ref, q_ref, out_ref):
    got = dot1(p_ref[...], q_ref[...], TN)
    out_ref[:, :ROWS, :] = got[:, :H].reshape(VOX, ROWS, H)
    out_ref[:, ROWS:, :] = got[:, H:].reshape(VOX, ROWS, H)


def cross_gram(p, q):
    return pl.pallas_call(
        cross_gram_kernel,
        out_shape=jax.ShapeDtypeStruct((VOX, 2 * ROWS, H), F32),
        in_specs=[VMEM, VMEM],
        out_specs=VMEM,
        compiler_params=params(6),
        name="cross_gram",
    )(p, q)


def rows_kernel(parts_ref, w_ref, out_ref):
    total = jnp.sum(parts_ref[...].astype(F32), axis=0)
    hi, lo = split(total)
    got = jnp.zeros((ROWS, N), F32)
    for k in range(2):
        at = slice(N * k, N * (k + 1))
        got = got + (dot1(hi[:, at], w_ref[k], NT) + dot1(lo[:, at], w_ref[k], NT))
    out_ref[...] = jnp.broadcast_to(got.astype(BF16)[None], out_ref.shape)


def cross_rows_of(parts, w):
    return pl.pallas_call(
        rows_kernel,
        out_shape=jax.ShapeDtypeStruct((VOX, ROWS, N), BF16),
        in_specs=[VMEM, VMEM],
        out_specs=VMEM,
        compiler_params=params(4),
        name="cross_rows",
    )(parts, w)


def partner(value, mask):
    return lax.ppermute(value, "grp", [(g, g ^ mask) for g in range(GRP)])


def exchange(parts):
    return lax.all_to_all(parts, "vox", 0, 0)


def same_core(rows):
    groups = [[2 * y + c for y in range(8)] for c in range(2)]
    sent = jnp.broadcast_to(rows[None], (8,) + rows.shape)
    return lax.all_to_all(sent, "vox", 0, 0, axis_index_groups=groups)


def swap_cores(value):
    return lax.ppermute(value, "vox", [(v, v ^ 1) for v in range(VOX)])


def add_up(parts):
    return jnp.sum(parts.astype(F32), axis=0)


def tree(own, series):
    core = (lax.axis_index("vox") & 1).astype(jnp.int32).reshape(1)
    other = partner(own, 1)
    own_rows = add_up(exchange(self_gram(own)))
    far_own = partner(own, 3)
    far_other = partner(other, 3)
    other_rows = partner(own_rows, 1)
    cross_rows = add_up(exchange(cross_gram(own, other)))
    rows = jnp.concatenate([own_rows, other_rows, cross_rows], axis=0)
    mine = same_core(rows)
    theirs = swap_cores(mine)
    w = full_weights(core, mine, theirs)

    left, parts = project(own, other, w, far_own, far_other)
    parts = exchange(parts)
    far_w = partner(w, 3)
    deep_left = partner(left, 4)
    cross = exchange(cross_rows_of(parts, far_w))
    right = mix(far_own, far_other, far_w)
    deep_right = partner(right, 4)
    w = plain_weights(cross.reshape(N, N))

    left, parts = project(left, right, w, deep_left, deep_right)
    parts = exchange(parts)
    deep_w = partner(w, 4)
    cross = exchange(cross_rows_of(parts, deep_w))
    right = mix(deep_left, deep_right, deep_w)
    w = plain_weights(cross.reshape(N, N))

    parts = load(left, right, w, series)
    return add_up(exchange(parts))


def local(group_basis, timeseries):
    return tree(group_basis[0], timeseries[0])[None]


def solution(mesh):
    return jax.shard_map(
        local,
        mesh=mesh,
        in_specs=(P("grp", "vox", None), P("grp", "vox", None)),
        out_specs=P("grp", "vox", None),
        check_vma=False,
    )
```

```python
import functools

import jax
import jax.numpy as jnp
from jax import lax
from jax.experimental import pallas as pl
from jax.experimental.pallas import tpu as pltpu
from jax.sharding import PartitionSpec as P


N = 256
H = 128
VOX = 16
GRP = 32
ROWS = N // VOX
F32 = jnp.float32
BF16 = jnp.bfloat16

NN = (((1,), (0,)), ((), ()))
NT = (((1,), (1,)), ((), ()))
TN = (((0,), (0,)), ((), ()))
VMEM = pl.BlockSpec(memory_space=pltpu.VMEM)
SMEM = pl.BlockSpec(memory_space=pltpu.SMEM)
HBM = pl.BlockSpec(memory_space=pltpu.MemorySpace.HBM)


def params(mib):
    return pltpu.CompilerParams(vmem_limit_bytes=mib << 20)


def dot1(a, b, dims):
    return lax.dot_general(a.astype(BF16), b.astype(BF16), dims, preferred_element_type=F32)


def split(x):
    hi = x.astype(BF16)
    return hi, (x - hi.astype(F32)).astype(BF16)


def dot3(a, b, dims):
    dot = functools.partial(lax.dot_general, dimension_numbers=dims, preferred_element_type=F32)
    return dot(a[0], b[0]) + (dot(a[0], b[1]) + dot(a[1], b[0]))


def dot_full(a, b, dims):
    return lax.dot_general(a, b, dims, preferred_element_type=F32, precision=lax.Precision.HIGHEST)


def iotas():
    shape = (N, N)
    return lax.broadcasted_iota(jnp.int32, shape, 0), lax.broadcasted_iota(jnp.int32, shape, 1)


def inv_sqrt_diag(m, eye):
    picked = jnp.where(eye, m, 0.0)
    col = lax.rsqrt(jnp.sum(picked, axis=1, keepdims=True))
    row = lax.rsqrt(jnp.sum(picked, axis=0, keepdims=True))
    return col, row


def inverse_factor(m):
    r, c = iotas()
    eye = r == c
    below = r > c
    one = jnp.where(eye, 1.0, 0.0)
    col, start = inv_sqrt_diag(m, eye)
    m = col * m * start
    s = jnp.where(below, m, 0.0)
    s2 = dot1(s, s, NN)
    t = one - s
    x = t + dot1(t, s2, NN)
    for _ in range(2):
        mk = dot1(dot1(x, m, NN), x, NT)
        col, row = inv_sqrt_diag(mk, eye)
        s = jnp.where(below, col * mk * row, 0.0)
        s2 = dot1(s, s, NN)
        t = one - s
        x = col * x
        x = x - dot1(s, x, NN) + dot1(dot1(t, s2, NN), x, NN)
    x = jnp.where(r >= c, x, 0.0)
    xs = split(x)
    mk = dot3(split(dot3(xs, split(m), NN)), xs, NT)
    col, row = inv_sqrt_diag(mk, eye)
    off = jnp.where(eye, 0.0, col * mk * row)
    size = jnp.sum(off * off)
    s = jnp.where(below, off, 0.0)
    x = col * x
    step = s - dot1(s, s, NN)
    x = x - dot3(split(step), split(x), NN)
    return x * start, size


def factor_columns(m_ref, l_ref):
    r, c = iotas()

    def body(j, _):
        m = m_ref[...]
        row = jnp.sum(jnp.where(r == j, m, 0.0), axis=0, keepdims=True)
        col = jnp.sum(jnp.where(c == j, m, 0.0), axis=1, keepdims=True)
        pivot = jnp.sum(jnp.where((r == j) & (c == j), m, 0.0))
        pivot = jnp.full((1, N), pivot, F32)
        row = jnp.where(c[:1] >= j, row, 0.0)
        col = jnp.where(r[:, :1] >= j, col, 0.0)
        m_ref[...] = m - col * (row / pivot)
        l_ref[...] = jnp.where(c == j, col / jnp.sqrt(pivot), l_ref[...])
        return 0

    lax.fori_loop(0, N, body, 0)


def invert_lower(l_ref, x_ref):
    r, c = iotas()
    eye = r == c
    diag = jnp.sum(jnp.where(eye, l_ref[...], 0.0), axis=1, keepdims=True)
    x_ref[...] = jnp.where(eye, 1.0 / diag, 0.0)

    def body(k, _):
        rk, ck = r >> k, c >> k
        off = jnp.where(((rk >> 1) == (ck >> 1)) & (rk > ck), l_ref[...], 0.0)
        x = x_ref[...]
        x_ref[...] = x - dot_full(dot_full(x, off, NN), x, NN)
        return 0

    lax.fori_loop(0, 8, body, 0)


def weights_body(a, b, cross, out_ref, y_ref, z_ref, m_ref, l_ref):
    plain = a is None
    r, c = iotas()
    if plain:
        one = jnp.where(r == c, 1.0, 0.0)
        t0, t1 = one + cross.T, one + cross
        unscale = 1.0
    else:
        top = jnp.max(jnp.where(r == c, jnp.maximum(a, b), 0.0))
        top = jnp.full((1, N), top, F32)
        inv = 1.0 / top
        unscale = lax.rsqrt(top)
        a, b, cross = a * inv, b * inv, cross * inv
        sa, sb, sc = split(a), split(b), split(cross)
        t0, t1 = a + cross.T, b + cross

    def times(t0, t1):
        s0, s1 = split(t0), split(t1)
        if plain:
            left = dot1(s1[0], cross, NT) + dot1(s1[1], cross, NT)
            right = dot1(s0[0], cross, NN) + dot1(s0[1], cross, NN)
            return t0 + left, t1 + right
        left, right = dot3(s1, sc, NT), dot3(s0, sc, NN)
        return dot3(s0, sa, NN) + left, dot3(s1, sb, NN) + right

    u0, u1 = times(t0, t1)
    v0, v1 = times(u0, u1)
    us0, us1 = split(u0), split(u1)
    m = dot3(split(v0), us0, NT) + dot3(split(v1), us1, NT)
    x, size = inverse_factor(m)
    xs = split(x)
    out_ref[0] = (dot3(xs, us0, NN) * unscale).astype(BF16)
    out_ref[1] = (dot3(xs, us1, NN) * unscale).astype(BF16)
    good = jnp.where(size < 0.01, 1, 0)

    @pl.when(good == 0)
    def _():
        y_ref[0] = t0
        y_ref[1] = t1

        def step(it, _):
            y0, y1 = y_ref[0], y_ref[1]
            left, right = dot_full(y1, cross, NT), dot_full(y0, cross, NN)
            if plain:
                z0, z1 = y0 + left, y1 + right
            else:
                z0, z1 = dot_full(y0, a, NN) + left, dot_full(y1, b, NN) + right
            m_ref[...] = dot_full(z0, y0, NT) + dot_full(z1, y1, NT)
            z_ref[0] = jnp.where(it == 0, z0, y0)
            z_ref[1] = jnp.where(it == 0, z1, y1)
            l_ref[...] = jnp.zeros((N, N), F32)
            factor_columns(m_ref, l_ref)
            invert_lower(l_ref, m_ref)
            xi = m_ref[...]
            y_ref[0] = dot_full(xi, z_ref[0], NN)
            y_ref[1] = dot_full(xi, z_ref[1], NN)
            return 0

        lax.fori_loop(0, 2, step, 0)
        out_ref[0] = (y_ref[0] * unscale).astype(BF16)
        out_ref[1] = (y_ref[1] * unscale).astype(BF16)


SCRATCH = [pltpu.VMEM((2, N, N), F32)] * 2 + [pltpu.VMEM((N, N), F32)] * 2
WEIGHTS = jax.ShapeDtypeStruct((2, N, N), BF16)


def full_kernel(core_ref, mine_ref, theirs_ref, out_ref, a_ref, c_ref, *scratch):
    core = core_ref[0]
    for half, ref in ((core, mine_ref), (1 - core, theirs_ref)):
        for y in range(8):
            block = 2 * y + half
            lo = pl.ds(pl.multiple_of(8 * block, 8), 8)
            hi = pl.ds(pl.multiple_of(H + 8 * block, 8), 8)
            for k in range(2):
                a_ref[k, lo, :H] = ref[y, 24 * k : 24 * k + 8, :]
                a_ref[k, hi, H:] = ref[y, 24 * k + 8 : 24 * k + 16, :]
                a_ref[k, hi, :H] = ref[y, 24 * k + 16 : 24 * k + 24, :]
            at = pl.ds(pl.multiple_of(ROWS * block, ROWS), ROWS)
            c_ref[at, :H] = ref[y, 48:64, :]
            c_ref[at, H:] = ref[y, 64:80, :]
    for k in range(2):
        a_ref[k, :H, H:] = a_ref[k, H:, :H].T
    weights_body(a_ref[0], a_ref[1], c_ref[...], out_ref, *scratch)


def full_weights(core, mine, theirs):
    return pl.pallas_call(
        full_kernel,
        out_shape=WEIGHTS,
        in_specs=[SMEM, VMEM, VMEM],
        out_specs=VMEM,
        scratch_shapes=[pltpu.VMEM((2, N, N), F32), pltpu.VMEM((N, N), F32)] + SCRATCH,
        compiler_params=params(12),
        name="full_weights",
    )(core, mine, theirs)


def plain_kernel(cross_ref, out_ref, *scratch):
    weights_body(None, None, cross_ref[...].astype(F32), out_ref, *scratch)


def plain_weights(cross):
    return pl.pallas_call(
        plain_kernel,
        out_shape=WEIGHTS,
        in_specs=[VMEM],
        out_specs=VMEM,
        scratch_shapes=SCRATCH,
        compiler_params=params(12),
        name="plain_weights",
    )(cross)


def mix_kernel(p_ref, q_ref, w_ref, out_ref):
    out = dot1(p_ref[...], w_ref[0], NT) + dot1(q_ref[...], w_ref[1], NT)
    out_ref[...] = out.astype(BF16)


def mix(p, q, w):
    return pl.pallas_call(
        mix_kernel,
        out_shape=jax.ShapeDtypeStruct(p.shape, BF16),
        in_specs=[VMEM] * 3,
        out_specs=VMEM,
        compiler_params=params(6),
        name="mix",
    )(p, q, w)


def project_kernel(p_ref, q_ref, w_ref, r_ref, s_ref, out_hbm, proj_ref, out_ref, sem):
    out = dot1(p_ref[...], w_ref[0], NT) + dot1(q_ref[...], w_ref[1], NT)
    out = out.astype(BF16)
    out_ref[...] = out
    copy = pltpu.make_async_copy(out_ref, out_hbm, sem)
    copy.start()
    for k, side in enumerate((r_ref, s_ref)):
        got = dot1(out, side[...], TN).astype(BF16)
        proj_ref[:, :, N * k : N * (k + 1)] = got.reshape(VOX, ROWS, N)
    copy.wait()


def project(p, q, w, r, s):
    return pl.pallas_call(
        project_kernel,
        out_shape=(
            jax.ShapeDtypeStruct(p.shape, BF16),
            jax.ShapeDtypeStruct((VOX, ROWS, 2 * N), BF16),
        ),
        in_specs=[VMEM] * 5,
        out_specs=(HBM, VMEM),
        scratch_shapes=[pltpu.VMEM(p.shape, BF16), pltpu.SemaphoreType.DMA],
        compiler_params=params(8),
        name="project",
    )(p, q, w, r, s)


def load_kernel(p_hbm, q_ref, w_ref, series_ref, out_ref, p_ref, sem):
    copy = pltpu.make_async_copy(p_hbm, p_ref, sem)
    copy.start()
    root = dot1(q_ref[...], w_ref[1], NT)
    copy.wait()
    root = (root + dot1(p_ref[...], w_ref[0], NT)).astype(BF16)
    got = dot1(root, series_ref[...], TN).astype(BF16)
    out_ref[...] = got.reshape(out_ref.shape)


def load(p, q, w, series):
    return pl.pallas_call(
        load_kernel,
        out_shape=jax.ShapeDtypeStruct((VOX, ROWS, series.shape[1]), BF16),
        in_specs=[HBM, VMEM, VMEM, VMEM],
        out_specs=VMEM,
        scratch_shapes=[pltpu.VMEM(p.shape, BF16), pltpu.SemaphoreType.DMA],
        compiler_params=params(8),
        name="load",
    )(p, q, w, series)


def self_gram_kernel(p_hbm, out_ref, p_ref, sems):
    half = p_hbm.shape[0] // 2
    copies = []
    for k in range(2):
        at = pl.ds(half * k, half)
        copies.append(pltpu.make_async_copy(p_hbm.at[at], p_ref.at[at], sems.at[k]))
        copies[-1].start()
    total = None
    for k in range(2):
        copies[k].wait()
        at = pl.ds(half * k, half)
        left, right = p_ref[at, :H], p_ref[at, H:]
        pairs = ((left, left), (right, right), (right, left))
        got = [dot1(a, b, TN) for a, b in pairs]
        total = got if total is None else [x + y for x, y in zip(total, got)]
    for k in range(3):
        out_ref[:, 8 * k : 8 * k + 8, :] = total[k].reshape(VOX, 8, H)


def self_gram(p):
    return pl.pallas_call(
        self_gram_kernel,
        out_shape=jax.ShapeDtypeStruct((VOX, 24, H), F32),
        in_specs=[HBM],
        out_specs=VMEM,
        scratch_shapes=[pltpu.VMEM(p.shape, BF16), pltpu.SemaphoreType.DMA((2,))],
        compiler_params=params(4),
        name="self_gram",
    )(pltpu.with_memory_space_constraint(p, pltpu.MemorySpace.HBM))


def cross_gram_kernel(p_ref, q_ref, out_ref):
    got = dot1(p_ref[...], q_ref[...], TN)
    out_ref[:, :ROWS, :] = got[:, :H].reshape(VOX, ROWS, H)
    out_ref[:, ROWS:, :] = got[:, H:].reshape(VOX, ROWS, H)


def cross_gram(p, q):
    return pl.pallas_call(
        cross_gram_kernel,
        out_shape=jax.ShapeDtypeStruct((VOX, 2 * ROWS, H), F32),
        in_specs=[VMEM, VMEM],
        out_specs=VMEM,
        compiler_params=params(6),
        name="cross_gram",
    )(p, q)


def rows_kernel(parts_ref, w_ref, out_ref):
    total = jnp.sum(parts_ref[...].astype(F32), axis=0)
    hi, lo = split(total)
    got = jnp.zeros((ROWS, N), F32)
    for k in range(2):
        at = slice(N * k, N * (k + 1))
        got = got + (dot1(hi[:, at], w_ref[k], NT) + dot1(lo[:, at], w_ref[k], NT))
    out_ref[...] = jnp.broadcast_to(got.astype(BF16)[None], out_ref.shape)


def cross_rows_of(parts, w):
    return pl.pallas_call(
        rows_kernel,
        out_shape=jax.ShapeDtypeStruct((VOX, ROWS, N), BF16),
        in_specs=[VMEM, VMEM],
        out_specs=VMEM,
        compiler_params=params(4),
        name="cross_rows",
    )(parts, w)


def partner(value, mask):
    return lax.ppermute(value, "grp", [(g, g ^ mask) for g in range(GRP)])


def exchange(parts):
    return lax.all_to_all(parts, "vox", 0, 0)


def same_core(rows):
    groups = [[2 * y + c for y in range(8)] for c in range(2)]
    sent = jnp.broadcast_to(rows[None], (8,) + rows.shape)
    return lax.all_to_all(sent, "vox", 0, 0, axis_index_groups=groups)


def swap_cores(value):
    return lax.ppermute(value, "vox", [(v, v ^ 1) for v in range(VOX)])


def add_up(parts):
    return jnp.sum(parts.astype(F32), axis=0)


def tree(own, series):
    core = (lax.axis_index("vox") & 1).astype(jnp.int32).reshape(1)
    other = partner(own, 1)
    own_rows = add_up(exchange(self_gram(own)))
    far_own = partner(own, 3)
    far_other = partner(other, 3)
    other_rows = partner(own_rows, 1)
    cross_rows = add_up(exchange(cross_gram(own, other)))
    rows = jnp.concatenate([own_rows, other_rows, cross_rows], axis=0)
    mine = same_core(rows)
    theirs = swap_cores(mine)
    w = full_weights(core, mine, theirs)

    left, parts = project(own, other, w, far_own, far_other)
    parts = exchange(parts)
    far_w = partner(w, 3)
    deep_left = partner(left, 4)
    deep_right = partner(left, 7)
    cross = exchange(cross_rows_of(parts, far_w))
    right = mix(far_own, far_other, far_w)
    w = plain_weights(cross.reshape(N, N))

    left, parts = project(left, right, w, deep_left, deep_right)
    parts = exchange(parts)
    deep_w = partner(w, 4)
    cross = exchange(cross_rows_of(parts, deep_w))
    right = mix(deep_left, deep_right, deep_w)
    w = plain_weights(cross.reshape(N, N))

    parts = load(left, right, w, series)
    return add_up(exchange(parts))


def local(group_basis, timeseries):
    return tree(group_basis[0], timeseries[0])[None]


def solution(mesh):
    return jax.shard_map(
        local,
        mesh=mesh,
        in_specs=(P("grp", "vox", None), P("grp", "vox", None)),
        out_specs=P("grp", "vox", None),
        check_vma=False,
    )
```

```python
import functools

import jax
import jax.numpy as jnp
from jax import lax
from jax.experimental import pallas as pl
from jax.experimental.pallas import tpu as pltpu
from jax.sharding import PartitionSpec as P


N = 256
H = 128
VOX = 16
GRP = 32
ROWS = N // VOX
F32 = jnp.float32
BF16 = jnp.bfloat16

NN = (((1,), (0,)), ((), ()))
NT = (((1,), (1,)), ((), ()))
TN = (((0,), (0,)), ((), ()))
VMEM = pl.BlockSpec(memory_space=pltpu.VMEM)
SMEM = pl.BlockSpec(memory_space=pltpu.SMEM)
HBM = pl.BlockSpec(memory_space=pltpu.MemorySpace.HBM)


def params(mib):
    return pltpu.CompilerParams(vmem_limit_bytes=mib << 20)


def dot1(a, b, dims):
    return lax.dot_general(a.astype(BF16), b.astype(BF16), dims, preferred_element_type=F32)


def split(x):
    hi = x.astype(BF16)
    return hi, (x - hi.astype(F32)).astype(BF16)


def dot3(a, b, dims):
    dot = functools.partial(lax.dot_general, dimension_numbers=dims, preferred_element_type=F32)
    return dot(a[0], b[0]) + (dot(a[0], b[1]) + dot(a[1], b[0]))


def dot_full(a, b, dims):
    return lax.dot_general(a, b, dims, preferred_element_type=F32, precision=lax.Precision.HIGHEST)


def iotas():
    shape = (N, N)
    return lax.broadcasted_iota(jnp.int32, shape, 0), lax.broadcasted_iota(jnp.int32, shape, 1)


def inv_sqrt_diag(m, eye):
    picked = jnp.where(eye, m, 0.0)
    col = lax.rsqrt(jnp.sum(picked, axis=1, keepdims=True))
    row = lax.rsqrt(jnp.sum(picked, axis=0, keepdims=True))
    return col, row


def inverse_factor(m, steps):
    r, c = iotas()
    eye = r == c
    below = r > c
    one = jnp.where(eye, 1.0, 0.0)
    col, start = inv_sqrt_diag(m, eye)
    m = col * m * start
    s = jnp.where(below, m, 0.0)
    s2 = dot1(s, s, NN)
    t = one - s
    x = t + dot1(t, s2, NN)
    for _ in range(steps):
        mk = dot1(dot1(x, m, NN), x, NT)
        col, row = inv_sqrt_diag(mk, eye)
        s = jnp.where(below, col * mk * row, 0.0)
        s2 = dot1(s, s, NN)
        t = one - s
        x = col * x
        x = x - dot1(s, x, NN) + dot1(dot1(t, s2, NN), x, NN)
    x = jnp.where(r >= c, x, 0.0)
    xs = split(x)
    mk = dot3(split(dot3(xs, split(m), NN)), xs, NT)
    col, row = inv_sqrt_diag(mk, eye)
    off = jnp.where(eye, 0.0, col * mk * row)
    size = jnp.sum(off * off)
    s = jnp.where(below, off, 0.0)
    x = col * x
    step = s - dot1(s, s, NN)
    x = x - dot3(split(step), split(x), NN)
    return x * start, size


def factor_columns(m_ref, l_ref):
    r, c = iotas()

    def body(j, _):
        m = m_ref[...]
        row = jnp.sum(jnp.where(r == j, m, 0.0), axis=0, keepdims=True)
        col = jnp.sum(jnp.where(c == j, m, 0.0), axis=1, keepdims=True)
        pivot = jnp.sum(jnp.where((r == j) & (c == j), m, 0.0))
        pivot = jnp.full((1, N), pivot, F32)
        row = jnp.where(c[:1] >= j, row, 0.0)
        col = jnp.where(r[:, :1] >= j, col, 0.0)
        m_ref[...] = m - col * (row / pivot)
        l_ref[...] = jnp.where(c == j, col / jnp.sqrt(pivot), l_ref[...])
        return 0

    lax.fori_loop(0, N, body, 0)


def invert_lower(l_ref, x_ref):
    r, c = iotas()
    eye = r == c
    diag = jnp.sum(jnp.where(eye, l_ref[...], 0.0), axis=1, keepdims=True)
    x_ref[...] = jnp.where(eye, 1.0 / diag, 0.0)

    def body(k, _):
        rk, ck = r >> k, c >> k
        off = jnp.where(((rk >> 1) == (ck >> 1)) & (rk > ck), l_ref[...], 0.0)
        x = x_ref[...]
        x_ref[...] = x - dot_full(dot_full(x, off, NN), x, NN)
        return 0

    lax.fori_loop(0, 8, body, 0)


def weights_body(a, b, cross, out_ref, y_ref, z_ref, m_ref, l_ref):
    plain = a is None
    r, c = iotas()
    if plain:
        one = jnp.where(r == c, 1.0, 0.0)
        t0, t1 = one + cross.T, one + cross
        unscale = 1.0
    else:
        top = jnp.max(jnp.where(r == c, jnp.maximum(a, b), 0.0))
        top = jnp.full((1, N), top, F32)
        inv = 1.0 / top
        unscale = lax.rsqrt(top)
        a, b, cross = a * inv, b * inv, cross * inv
        sa, sb, sc = split(a), split(b), split(cross)
        t0, t1 = a + cross.T, b + cross

    def times(t0, t1):
        s0, s1 = split(t0), split(t1)
        if plain:
            left = dot1(s1[0], cross, NT) + dot1(s1[1], cross, NT)
            right = dot1(s0[0], cross, NN) + dot1(s0[1], cross, NN)
            return t0 + left, t1 + right
        left, right = dot3(s1, sc, NT), dot3(s0, sc, NN)
        return dot3(s0, sa, NN) + left, dot3(s1, sb, NN) + right

    u0, u1 = times(t0, t1)
    v0, v1 = times(u0, u1)
    us0, us1 = split(u0), split(u1)
    m = dot3(split(v0), us0, NT) + dot3(split(v1), us1, NT)
    x, size = inverse_factor(m, 1 if plain else 2)
    xs = split(x)
    out_ref[0] = (dot3(xs, us0, NN) * unscale).astype(BF16)
    out_ref[1] = (dot3(xs, us1, NN) * unscale).astype(BF16)
    good = jnp.where(size < 0.06, 1, 0)

    @pl.when(good == 0)
    def _():
        y_ref[0] = t0
        y_ref[1] = t1

        def step(it, _):
            y0, y1 = y_ref[0], y_ref[1]
            left, right = dot_full(y1, cross, NT), dot_full(y0, cross, NN)
            if plain:
                z0, z1 = y0 + left, y1 + right
            else:
                z0, z1 = dot_full(y0, a, NN) + left, dot_full(y1, b, NN) + right
            m_ref[...] = dot_full(z0, y0, NT) + dot_full(z1, y1, NT)
            z_ref[0] = jnp.where(it == 0, z0, y0)
            z_ref[1] = jnp.where(it == 0, z1, y1)
            l_ref[...] = jnp.zeros((N, N), F32)
            factor_columns(m_ref, l_ref)
            invert_lower(l_ref, m_ref)
            xi = m_ref[...]
            y_ref[0] = dot_full(xi, z_ref[0], NN)
            y_ref[1] = dot_full(xi, z_ref[1], NN)
            return 0

        lax.fori_loop(0, 2, step, 0)
        out_ref[0] = (y_ref[0] * unscale).astype(BF16)
        out_ref[1] = (y_ref[1] * unscale).astype(BF16)


def mixed(p_ref, q_ref, w_ref):
    out = dot1(p_ref[...], w_ref[0], NT) + dot1(q_ref[...], w_ref[1], NT)
    return out.astype(BF16)


def project_into(node, sides, proj_ref):
    for k, side in enumerate(sides):
        got = dot1(node, side[...], TN).astype(BF16)
        proj_ref[:, :, N * k : N * (k + 1)] = got.reshape(VOX, ROWS, N)


SCRATCH = [pltpu.VMEM((2, N, N), F32)] * 2 + [pltpu.VMEM((N, N), F32)] * 2
WEIGHTS = jax.ShapeDtypeStruct((2, N, N), BF16)


def full_kernel(core_ref, mine_ref, theirs_ref, p_ref, q_ref, r_ref, s_ref, *refs):
    out_ref, node_hbm, proj_ref, a_ref, c_ref, node_ref, sem = refs[:7]
    core = core_ref[0]
    for half, ref in ((core, mine_ref), (1 - core, theirs_ref)):
        for y in range(8):
            block = 2 * y + half
            lo = pl.ds(pl.multiple_of(8 * block, 8), 8)
            hi = pl.ds(pl.multiple_of(H + 8 * block, 8), 8)
            for k in range(2):
                a_ref[k, lo, :H] = ref[y, 24 * k : 24 * k + 8, :]
                a_ref[k, hi, H:] = ref[y, 24 * k + 8 : 24 * k + 16, :]
                a_ref[k, hi, :H] = ref[y, 24 * k + 16 : 24 * k + 24, :]
            at = pl.ds(pl.multiple_of(ROWS * block, ROWS), ROWS)
            c_ref[at, :H] = ref[y, 48:64, :]
            c_ref[at, H:] = ref[y, 64:80, :]
    for k in range(2):
        a_ref[k, :H, H:] = a_ref[k, H:, :H].T
    weights_body(a_ref[0], a_ref[1], c_ref[...], out_ref, *refs[7:])
    node = mixed(p_ref, q_ref, out_ref)
    node_ref[...] = node
    copy = pltpu.make_async_copy(node_ref, node_hbm, sem)
    copy.start()
    project_into(node, (r_ref, s_ref), proj_ref)
    copy.wait()


def projections(node):
    parts = jax.ShapeDtypeStruct((VOX, ROWS, 2 * N), BF16)
    return jax.ShapeDtypeStruct(node.shape, BF16), parts


def full_merge(core, mine, theirs, p, q, r, s):
    return pl.pallas_call(
        full_kernel,
        out_shape=(WEIGHTS,) + projections(p),
        in_specs=[SMEM] + [VMEM] * 6,
        out_specs=(VMEM, HBM, VMEM),
        scratch_shapes=[pltpu.VMEM((2, N, N), F32), pltpu.VMEM((N, N), F32)]
        + [pltpu.VMEM(p.shape, BF16), pltpu.SemaphoreType.DMA]
        + SCRATCH,
        compiler_params=params(16),
        name="full_merge",
    )(core, mine, theirs, p, q, r, s)


def plain_kernel(cross_ref, out_ref, *scratch):
    weights_body(None, None, cross_ref[...].astype(F32), out_ref, *scratch)


def plain_weights(cross):
    return pl.pallas_call(
        plain_kernel,
        out_shape=WEIGHTS,
        in_specs=[VMEM],
        out_specs=VMEM,
        scratch_shapes=SCRATCH,
        compiler_params=params(12),
        name="plain_weights",
    )(cross)


def mix_kernel(p_ref, q_ref, w_ref, out_ref):
    out_ref[...] = mixed(p_ref, q_ref, w_ref)


def mix(p, q, w):
    return pl.pallas_call(
        mix_kernel,
        out_shape=jax.ShapeDtypeStruct(p.shape, BF16),
        in_specs=[VMEM] * 3,
        out_specs=VMEM,
        compiler_params=params(6),
        name="mix",
    )(p, q, w)


def project_kernel(p_ref, q_ref, w_ref, r_ref, s_ref, out_hbm, proj_ref, out_ref, sem):
    out = mixed(p_ref, q_ref, w_ref)
    out_ref[...] = out
    copy = pltpu.make_async_copy(out_ref, out_hbm, sem)
    copy.start()
    project_into(out, (r_ref, s_ref), proj_ref)
    copy.wait()


def project(p, q, w, r, s):
    return pl.pallas_call(
        project_kernel,
        out_shape=projections(p),
        in_specs=[VMEM] * 5,
        out_specs=(HBM, VMEM),
        scratch_shapes=[pltpu.VMEM(p.shape, BF16), pltpu.SemaphoreType.DMA],
        compiler_params=params(8),
        name="project",
    )(p, q, w, r, s)


def last_kernel(cross_ref, p_hbm, q_ref, series_hbm, out_ref, *refs):
    p_ref, series_ref, p_sem, series_sem, w_ref = refs[:5]
    first = pltpu.make_async_copy(p_hbm, p_ref, p_sem)
    first.start()
    second = pltpu.make_async_copy(series_hbm, series_ref, series_sem)
    second.start()
    weights_body(None, None, cross_ref[...].astype(F32), w_ref, *refs[5:])
    first.wait()
    second.wait()
    root = mixed(p_ref, q_ref, w_ref)
    out_ref[...] = dot1(root, series_ref[...], TN).astype(BF16).reshape(out_ref.shape)


def last_merge(cross, p, q, series):
    return pl.pallas_call(
        last_kernel,
        out_shape=jax.ShapeDtypeStruct((VOX, ROWS, series.shape[1]), BF16),
        in_specs=[VMEM, HBM, VMEM, HBM],
        out_specs=VMEM,
        scratch_shapes=[pltpu.VMEM(p.shape, BF16), pltpu.VMEM(series.shape, BF16)]
        + [pltpu.SemaphoreType.DMA] * 2
        + [pltpu.VMEM((2, N, N), BF16)]
        + SCRATCH,
        compiler_params=params(16),
        name="last_merge",
    )(cross, p, q, pltpu.with_memory_space_constraint(series, pltpu.MemorySpace.HBM))


def self_gram_kernel(p_hbm, out_ref, p_ref, sems):
    half = p_hbm.shape[0] // 2
    copies = []
    for k in range(2):
        at = pl.ds(half * k, half)
        copies.append(pltpu.make_async_copy(p_hbm.at[at], p_ref.at[at], sems.at[k]))
        copies[-1].start()
    total = None
    for k in range(2):
        copies[k].wait()
        at = pl.ds(half * k, half)
        left, right = p_ref[at, :H], p_ref[at, H:]
        pairs = ((left, left), (right, right), (right, left))
        got = [dot1(a, b, TN) for a, b in pairs]
        total = got if total is None else [x + y for x, y in zip(total, got)]
    for k in range(3):
        out_ref[:, 8 * k : 8 * k + 8, :] = total[k].reshape(VOX, 8, H)


def self_gram(p):
    return pl.pallas_call(
        self_gram_kernel,
        out_shape=jax.ShapeDtypeStruct((VOX, 24, H), F32),
        in_specs=[HBM],
        out_specs=VMEM,
        scratch_shapes=[pltpu.VMEM(p.shape, BF16), pltpu.SemaphoreType.DMA((2,))],
        compiler_params=params(4),
        name="self_gram",
    )(pltpu.with_memory_space_constraint(p, pltpu.MemorySpace.HBM))


def cross_gram_kernel(p_ref, q_ref, out_ref):
    got = dot1(p_ref[...], q_ref[...], TN)
    out_ref[:, :ROWS, :] = got[:, :H].reshape(VOX, ROWS, H)
    out_ref[:, ROWS:, :] = got[:, H:].reshape(VOX, ROWS, H)


def cross_gram(p, q):
    return pl.pallas_call(
        cross_gram_kernel,
        out_shape=jax.ShapeDtypeStruct((VOX, 2 * ROWS, H), F32),
        in_specs=[VMEM, VMEM],
        out_specs=VMEM,
        compiler_params=params(6),
        name="cross_gram",
    )(p, q)


def rows_kernel(parts_ref, w_ref, out_ref):
    total = jnp.sum(parts_ref[...].astype(F32), axis=0)
    hi, lo = split(total)
    got = jnp.zeros((ROWS, N), F32)
    for k in range(2):
        at = slice(N * k, N * (k + 1))
        got = got + (dot1(hi[:, at], w_ref[k], NT) + dot1(lo[:, at], w_ref[k], NT))
    out_ref[...] = jnp.broadcast_to(got.astype(BF16)[None], out_ref.shape)


def cross_rows_of(parts, w):
    return pl.pallas_call(
        rows_kernel,
        out_shape=jax.ShapeDtypeStruct((VOX, ROWS, N), BF16),
        in_specs=[VMEM, VMEM],
        out_specs=VMEM,
        compiler_params=params(4),
        name="cross_rows",
    )(parts, w)


def partner(value, mask):
    return lax.ppermute(value, "grp", [(g, g ^ mask) for g in range(GRP)])


def exchange(parts):
    return lax.all_to_all(parts, "vox", 0, 0)


def same_core(rows):
    groups = [[2 * y + c for y in range(8)] for c in range(2)]
    sent = jnp.broadcast_to(rows[None], (8,) + rows.shape)
    return lax.all_to_all(sent, "vox", 0, 0, axis_index_groups=groups)


def swap_cores(value):
    return lax.ppermute(value, "vox", [(v, v ^ 1) for v in range(VOX)])


def add_up(parts):
    return jnp.sum(parts.astype(F32), axis=0)


def tree(own, series):
    core = (lax.axis_index("vox") & 1).astype(jnp.int32).reshape(1)
    other = partner(own, 1)
    own_rows = add_up(exchange(self_gram(own)))
    far_own = partner(own, 3)
    far_other = partner(other, 3)
    other_rows = partner(own_rows, 1)
    cross_rows = add_up(exchange(cross_gram(own, other)))
    rows = jnp.concatenate([own_rows, other_rows, cross_rows], axis=0)
    mine = same_core(rows)
    theirs = swap_cores(mine)
    w, left, parts = full_merge(core, mine, theirs, own, other, far_own, far_other)
    parts = exchange(parts)
    far_w = partner(w, 3)
    deep_left = partner(left, 4)
    deep_right = partner(left, 7)
    cross = exchange(cross_rows_of(parts, far_w))
    right = mix(far_own, far_other, far_w)
    w = plain_weights(cross.reshape(N, N))

    left, parts = project(left, right, w, deep_left, deep_right)
    parts = exchange(parts)
    deep_w = partner(w, 4)
    cross = exchange(cross_rows_of(parts, deep_w))
    right = mix(deep_left, deep_right, deep_w)
    parts = last_merge(cross.reshape(N, N), left, right, series)
    return add_up(exchange(parts))


def local(group_basis, timeseries):
    return tree(group_basis[0], timeseries[0])[None]


def solution(mesh):
    return jax.shard_map(
        local,
        mesh=mesh,
        in_specs=(P("grp", "vox", None), P("grp", "vox", None)),
        out_specs=P("grp", "vox", None),
        check_vma=False,
    )
```

```python
import functools

import jax
import jax.numpy as jnp
from jax import lax
from jax.experimental import pallas as pl
from jax.experimental.pallas import tpu as pltpu
from jax.sharding import PartitionSpec as P


N = 256
H = 128
VOX = 16
GRP = 32
ROWS = N // VOX
F32 = jnp.float32
BF16 = jnp.bfloat16

NN = (((1,), (0,)), ((), ()))
NT = (((1,), (1,)), ((), ()))
TN = (((0,), (0,)), ((), ()))
VMEM = pl.BlockSpec(memory_space=pltpu.VMEM)
SMEM = pl.BlockSpec(memory_space=pltpu.SMEM)
HBM = pl.BlockSpec(memory_space=pltpu.MemorySpace.HBM)


def params(mib):
    return pltpu.CompilerParams(vmem_limit_bytes=mib << 20)


def dot1(a, b, dims):
    return lax.dot_general(a.astype(BF16), b.astype(BF16), dims, preferred_element_type=F32)


def split(x):
    hi = x.astype(BF16)
    return hi, (x - hi.astype(F32)).astype(BF16)


def dot3(a, b, dims):
    dot = functools.partial(lax.dot_general, dimension_numbers=dims, preferred_element_type=F32)
    return dot(a[0], b[0]) + (dot(a[0], b[1]) + dot(a[1], b[0]))


def dot_full(a, b, dims):
    return lax.dot_general(a, b, dims, preferred_element_type=F32, precision=lax.Precision.HIGHEST)


def iotas():
    shape = (N, N)
    return lax.broadcasted_iota(jnp.int32, shape, 0), lax.broadcasted_iota(jnp.int32, shape, 1)


def inv_sqrt_diag(m, eye):
    picked = jnp.where(eye, m, 0.0)
    col = lax.rsqrt(jnp.sum(picked, axis=1, keepdims=True))
    row = lax.rsqrt(jnp.sum(picked, axis=0, keepdims=True))
    return col, row


def inverse_factor(m, steps):
    r, c = iotas()
    eye = r == c
    below = r > c
    one = jnp.where(eye, 1.0, 0.0)
    col, start = inv_sqrt_diag(m, eye)
    m = col * m * start
    s = jnp.where(below, m, 0.0)
    s2 = dot1(s, s, NN)
    t = one - s
    x = t + dot1(t, s2, NN)
    for _ in range(steps):
        mk = dot1(dot1(x, m, NN), x, NT)
        col, row = inv_sqrt_diag(mk, eye)
        s = jnp.where(below, col * mk * row, 0.0)
        s2 = dot1(s, s, NN)
        t = one - s
        x = col * x
        x = x - dot1(s, x, NN) + dot1(dot1(t, s2, NN), x, NN)
    x = jnp.where(r >= c, x, 0.0)
    xs = split(x)
    mk = dot3(split(dot3(xs, split(m), NN)), xs, NT)
    col, row = inv_sqrt_diag(mk, eye)
    off = jnp.where(eye, 0.0, col * mk * row)
    size = jnp.sum(off * off)
    s = jnp.where(below, off, 0.0)
    x = col * x
    step = s - dot1(s, s, NN)
    x = x - dot3(split(step), split(x), NN)
    return x * start, size


def factor_columns(m_ref, l_ref):
    r, c = iotas()

    def body(j, _):
        m = m_ref[...]
        row = jnp.sum(jnp.where(r == j, m, 0.0), axis=0, keepdims=True)
        col = jnp.sum(jnp.where(c == j, m, 0.0), axis=1, keepdims=True)
        pivot = jnp.sum(jnp.where((r == j) & (c == j), m, 0.0))
        pivot = jnp.full((1, N), pivot, F32)
        row = jnp.where(c[:1] >= j, row, 0.0)
        col = jnp.where(r[:, :1] >= j, col, 0.0)
        m_ref[...] = m - col * (row / pivot)
        l_ref[...] = jnp.where(c == j, col / jnp.sqrt(pivot), l_ref[...])
        return 0

    lax.fori_loop(0, N, body, 0)


def invert_lower(l_ref, x_ref):
    r, c = iotas()
    eye = r == c
    diag = jnp.sum(jnp.where(eye, l_ref[...], 0.0), axis=1, keepdims=True)
    x_ref[...] = jnp.where(eye, 1.0 / diag, 0.0)

    def body(k, _):
        rk, ck = r >> k, c >> k
        off = jnp.where(((rk >> 1) == (ck >> 1)) & (rk > ck), l_ref[...], 0.0)
        x = x_ref[...]
        x_ref[...] = x - dot_full(dot_full(x, off, NN), x, NN)
        return 0

    lax.fori_loop(0, 8, body, 0)


def weights_body(a, b, cross, out_ref, y_ref, z_ref, m_ref, l_ref):
    plain = a is None
    r, c = iotas()
    if plain:
        one = jnp.where(r == c, 1.0, 0.0)
        t0, t1 = one + cross.T, one + cross
        unscale = 1.0
    else:
        top = jnp.max(jnp.where(r == c, jnp.maximum(a, b), 0.0))
        top = jnp.full((1, N), top, F32)
        inv = 1.0 / top
        unscale = lax.rsqrt(top)
        a, b, cross = a * inv, b * inv, cross * inv
        sa, sb, sc = split(a), split(b), split(cross)
        t0, t1 = a + cross.T, b + cross

    def times(t0, t1):
        s0, s1 = split(t0), split(t1)
        if plain:
            left = dot1(s1[0], cross, NT) + dot1(s1[1], cross, NT)
            right = dot1(s0[0], cross, NN) + dot1(s0[1], cross, NN)
            return t0 + left, t1 + right
        left, right = dot3(s1, sc, NT), dot3(s0, sc, NN)
        return dot3(s0, sa, NN) + left, dot3(s1, sb, NN) + right

    u0, u1 = times(t0, t1)
    v0, v1 = times(u0, u1)
    us0, us1 = split(u0), split(u1)
    m = dot3(split(v0), us0, NT) + dot3(split(v1), us1, NT)
    x, size = inverse_factor(m, 1 if plain else 2)
    xs = split(x)
    out_ref[0] = (dot3(xs, us0, NN) * unscale).astype(BF16)
    out_ref[1] = (dot3(xs, us1, NN) * unscale).astype(BF16)
    good = jnp.where(size < 0.06, 1, 0)

    @pl.when(good == 0)
    def _():
        y_ref[0] = t0
        y_ref[1] = t1

        def step(it, _):
            y0, y1 = y_ref[0], y_ref[1]
            left, right = dot_full(y1, cross, NT), dot_full(y0, cross, NN)
            if plain:
                z0, z1 = y0 + left, y1 + right
            else:
                z0, z1 = dot_full(y0, a, NN) + left, dot_full(y1, b, NN) + right
            m_ref[...] = dot_full(z0, y0, NT) + dot_full(z1, y1, NT)
            z_ref[0] = jnp.where(it == 0, z0, y0)
            z_ref[1] = jnp.where(it == 0, z1, y1)
            l_ref[...] = jnp.zeros((N, N), F32)
            factor_columns(m_ref, l_ref)
            invert_lower(l_ref, m_ref)
            xi = m_ref[...]
            y_ref[0] = dot_full(xi, z_ref[0], NN)
            y_ref[1] = dot_full(xi, z_ref[1], NN)
            return 0

        lax.fori_loop(0, 2, step, 0)
        out_ref[0] = (y_ref[0] * unscale).astype(BF16)
        out_ref[1] = (y_ref[1] * unscale).astype(BF16)


def mixed(p_ref, q_ref, w_ref):
    out = dot1(p_ref[...], w_ref[0], NT) + dot1(q_ref[...], w_ref[1], NT)
    return out.astype(BF16)


def send_out(node, sides, node_hbm, proj_hbm, node_ref, proj_ref, sems):
    node_ref[...] = node
    copies = [pltpu.make_async_copy(node_ref, node_hbm, sems.at[0])]
    copies[0].start()
    for k, side in enumerate(sides):
        got = dot1(node, side[...], TN).astype(BF16)
        at = pl.ds(N * k, N)
        proj_ref[:, :, N * k : N * (k + 1)] = got.reshape(VOX, ROWS, N)
        copy = pltpu.make_async_copy(proj_ref.at[:, :, at], proj_hbm.at[:, :, at], sems.at[1 + k])
        copy.start()
        copies.append(copy)
    for copy in copies:
        copy.wait()


def sending(p):
    rows = pltpu.VMEM((VOX, ROWS, 2 * N), BF16)
    return [pltpu.VMEM(p.shape, BF16), rows, pltpu.SemaphoreType.DMA((3,))]


SCRATCH = [pltpu.VMEM((2, N, N), F32)] * 2 + [pltpu.VMEM((N, N), F32)] * 2
WEIGHTS = jax.ShapeDtypeStruct((2, N, N), BF16)


def full_kernel(core_ref, mine_ref, theirs_ref, p_ref, q_ref, r_ref, s_ref, *refs):
    out_ref, node_hbm, proj_hbm, a_ref, c_ref = refs[:5]
    core = core_ref[0]
    for half, ref in ((core, mine_ref), (1 - core, theirs_ref)):
        for y in range(8):
            block = 2 * y + half
            lo = pl.ds(pl.multiple_of(8 * block, 8), 8)
            hi = pl.ds(pl.multiple_of(H + 8 * block, 8), 8)
            for k in range(2):
                a_ref[k, lo, :H] = ref[y, 24 * k : 24 * k + 8, :]
                a_ref[k, hi, H:] = ref[y, 24 * k + 8 : 24 * k + 16, :]
                a_ref[k, hi, :H] = ref[y, 24 * k + 16 : 24 * k + 24, :]
            at = pl.ds(pl.multiple_of(ROWS * block, ROWS), ROWS)
            c_ref[at, :H] = ref[y, 48:64, :]
            c_ref[at, H:] = ref[y, 64:80, :]
    for k in range(2):
        a_ref[k, :H, H:] = a_ref[k, H:, :H].T
    weights_body(a_ref[0], a_ref[1], c_ref[...], out_ref, *refs[8:])
    node = mixed(p_ref, q_ref, out_ref)
    send_out(node, (r_ref, s_ref), node_hbm, proj_hbm, *refs[5:8])


def projections(node):
    parts = jax.ShapeDtypeStruct((VOX, ROWS, 2 * N), BF16)
    return jax.ShapeDtypeStruct(node.shape, BF16), parts


def full_merge(core, mine, theirs, p, q, r, s):
    return pl.pallas_call(
        full_kernel,
        out_shape=(WEIGHTS,) + projections(p),
        in_specs=[SMEM] + [VMEM] * 6,
        out_specs=(VMEM, HBM, HBM),
        scratch_shapes=[pltpu.VMEM((2, N, N), F32), pltpu.VMEM((N, N), F32)]
        + sending(p)
        + SCRATCH,
        compiler_params=params(16),
        name="full_merge",
    )(core, mine, theirs, p, q, r, s)


def plain_kernel(cross_ref, out_ref, *scratch):
    weights_body(None, None, cross_ref[...].astype(F32), out_ref, *scratch)


def plain_weights(cross):
    return pl.pallas_call(
        plain_kernel,
        out_shape=WEIGHTS,
        in_specs=[VMEM],
        out_specs=VMEM,
        scratch_shapes=SCRATCH,
        compiler_params=params(12),
        name="plain_weights",
    )(cross)


def mix_kernel(p_ref, q_ref, w_ref, out_ref):
    out_ref[...] = mixed(p_ref, q_ref, w_ref)


def mix(p, q, w):
    return pl.pallas_call(
        mix_kernel,
        out_shape=jax.ShapeDtypeStruct(p.shape, BF16),
        in_specs=[VMEM] * 3,
        out_specs=VMEM,
        compiler_params=params(6),
        name="mix",
    )(p, q, w)


def project_kernel(p_hbm, q_ref, w_ref, r_ref, s_ref, node_hbm, proj_hbm, p_ref, sem, *refs):
    copy = pltpu.make_async_copy(p_hbm, p_ref, sem)
    copy.start()
    node = dot1(q_ref[...], w_ref[1], NT)
    copy.wait()
    node = (node + dot1(p_ref[...], w_ref[0], NT)).astype(BF16)
    send_out(node, (r_ref, s_ref), node_hbm, proj_hbm, *refs)


def project(p, q, w, r, s):
    return pl.pallas_call(
        project_kernel,
        out_shape=projections(p),
        in_specs=[HBM] + [VMEM] * 4,
        out_specs=(HBM, HBM),
        scratch_shapes=[pltpu.VMEM(p.shape, BF16), pltpu.SemaphoreType.DMA] + sending(p),
        compiler_params=params(10),
        name="project",
    )(p, q, w, r, s)


def last_kernel(cross_ref, p_hbm, q_ref, series_hbm, out_ref, *refs):
    p_ref, series_ref, p_sem, series_sem, w_ref = refs[:5]
    first = pltpu.make_async_copy(p_hbm, p_ref, p_sem)
    first.start()
    second = pltpu.make_async_copy(series_hbm, series_ref, series_sem)
    second.start()
    weights_body(None, None, cross_ref[...].astype(F32), w_ref, *refs[5:])
    first.wait()
    second.wait()
    root = mixed(p_ref, q_ref, w_ref)
    out_ref[...] = dot1(root, series_ref[...], TN).astype(BF16).reshape(out_ref.shape)


def last_merge(cross, p, q, series):
    return pl.pallas_call(
        last_kernel,
        out_shape=jax.ShapeDtypeStruct((VOX, ROWS, series.shape[1]), BF16),
        in_specs=[VMEM, HBM, VMEM, HBM],
        out_specs=VMEM,
        scratch_shapes=[pltpu.VMEM(p.shape, BF16), pltpu.VMEM(series.shape, BF16)]
        + [pltpu.SemaphoreType.DMA] * 2
        + [pltpu.VMEM((2, N, N), BF16)]
        + SCRATCH,
        compiler_params=params(16),
        name="last_merge",
    )(cross, p, q, pltpu.with_memory_space_constraint(series, pltpu.MemorySpace.HBM))


def self_gram_kernel(p_hbm, out_ref, p_ref, sems):
    piece = p_hbm.shape[0] // 4
    copies = []
    for k in range(4):
        at = pl.ds(piece * k, piece)
        copies.append(pltpu.make_async_copy(p_hbm.at[at], p_ref.at[at], sems.at[k]))
        copies[-1].start()
    total = None
    for k in range(4):
        copies[k].wait()
        at = pl.ds(piece * k, piece)
        left, right = p_ref[at, :H], p_ref[at, H:]
        pairs = ((left, left), (right, right), (right, left))
        got = [dot1(a, b, TN) for a, b in pairs]
        total = got if total is None else [x + y for x, y in zip(total, got)]
    for k in range(3):
        out_ref[:, 8 * k : 8 * k + 8, :] = total[k].astype(BF16).reshape(VOX, 8, H)


def self_gram(p):
    return pl.pallas_call(
        self_gram_kernel,
        out_shape=jax.ShapeDtypeStruct((VOX, 24, H), BF16),
        in_specs=[HBM],
        out_specs=VMEM,
        scratch_shapes=[pltpu.VMEM(p.shape, BF16), pltpu.SemaphoreType.DMA((4,))],
        compiler_params=params(4),
        name="self_gram",
    )(pltpu.with_memory_space_constraint(p, pltpu.MemorySpace.HBM))


def cross_gram_kernel(p_ref, q_ref, out_ref):
    got = dot1(p_ref[...], q_ref[...], TN).astype(BF16)
    out_ref[:, :ROWS, :] = got[:, :H].reshape(VOX, ROWS, H)
    out_ref[:, ROWS:, :] = got[:, H:].reshape(VOX, ROWS, H)


def cross_gram(p, q):
    return pl.pallas_call(
        cross_gram_kernel,
        out_shape=jax.ShapeDtypeStruct((VOX, 2 * ROWS, H), BF16),
        in_specs=[VMEM, VMEM],
        out_specs=VMEM,
        compiler_params=params(6),
        name="cross_gram",
    )(p, q)


def rows_kernel(parts_ref, w_ref, out_ref):
    total = jnp.sum(parts_ref[...].astype(F32), axis=0)
    hi, lo = split(total)
    got = jnp.zeros((ROWS, N), F32)
    for k in range(2):
        at = slice(N * k, N * (k + 1))
        got = got + (dot1(hi[:, at], w_ref[k], NT) + dot1(lo[:, at], w_ref[k], NT))
    out_ref[...] = jnp.broadcast_to(got.astype(BF16)[None], out_ref.shape)


def cross_rows_of(parts, w):
    return pl.pallas_call(
        rows_kernel,
        out_shape=jax.ShapeDtypeStruct((VOX, ROWS, N), BF16),
        in_specs=[VMEM, VMEM],
        out_specs=VMEM,
        compiler_params=params(4),
        name="cross_rows",
    )(parts, w)


def partner(value, mask):
    return lax.ppermute(value, "grp", [(g, g ^ mask) for g in range(GRP)])


def exchange(parts):
    return lax.all_to_all(parts, "vox", 0, 0)


def same_core(rows):
    groups = [[2 * y + c for y in range(8)] for c in range(2)]
    sent = jnp.broadcast_to(rows[None], (8,) + rows.shape)
    return lax.all_to_all(sent, "vox", 0, 0, axis_index_groups=groups)


def swap_cores(value):
    return lax.ppermute(value, "vox", [(v, v ^ 1) for v in range(VOX)])


def add_up(parts):
    return jnp.sum(parts.astype(F32), axis=0)


def tree(own, series):
    core = (lax.axis_index("vox") & 1).astype(jnp.int32).reshape(1)
    other = partner(own, 1)
    own_rows = add_up(exchange(self_gram(own)))
    far_own = partner(own, 3)
    far_other = partner(other, 3)
    other_rows = partner(own_rows, 1)
    cross_rows = add_up(exchange(cross_gram(own, other)))
    rows = jnp.concatenate([own_rows, other_rows, cross_rows], axis=0)
    mine = same_core(rows)
    theirs = swap_cores(mine)
    w, left, parts = full_merge(core, mine, theirs, own, other, far_own, far_other)
    parts = exchange(parts)
    far_w = partner(w, 3)
    deep_left = partner(left, 4)
    deep_right = partner(left, 7)
    cross = exchange(cross_rows_of(parts, far_w))
    right = mix(far_own, far_other, far_w)
    w = plain_weights(cross.reshape(N, N))

    left, parts = project(left, right, w, deep_left, deep_right)
    parts = exchange(parts)
    deep_w = partner(w, 4)
    cross = exchange(cross_rows_of(parts, deep_w))
    right = mix(deep_left, deep_right, deep_w)
    parts = last_merge(cross.reshape(N, N), left, right, series)
    return add_up(exchange(parts))


def local(group_basis, timeseries):
    return tree(group_basis[0], timeseries[0])[None]


def solution(mesh):
    return jax.shard_map(
        local,
        mesh=mesh,
        in_specs=(P("grp", "vox", None), P("grp", "vox", None)),
        out_specs=P("grp", "vox", None),
        check_vma=False,
    )
```

```python
import functools

import jax
import jax.numpy as jnp
from jax import lax
from jax.experimental import pallas as pl
from jax.experimental.pallas import tpu as pltpu
from jax.sharding import PartitionSpec as P


N = 256
H = 128
VOX = 16
GRP = 32
ROWS = N // VOX
F32 = jnp.float32
BF16 = jnp.bfloat16

NN = (((1,), (0,)), ((), ()))
NT = (((1,), (1,)), ((), ()))
TN = (((0,), (0,)), ((), ()))
VMEM = pl.BlockSpec(memory_space=pltpu.VMEM)
SMEM = pl.BlockSpec(memory_space=pltpu.SMEM)
HBM = pl.BlockSpec(memory_space=pltpu.MemorySpace.HBM)


def params(mib):
    return pltpu.CompilerParams(vmem_limit_bytes=mib << 20)


def dot1(a, b, dims):
    return lax.dot_general(a.astype(BF16), b.astype(BF16), dims, preferred_element_type=F32)


def split(x):
    hi = x.astype(BF16)
    return hi, (x - hi.astype(F32)).astype(BF16)


def dot3(a, b, dims):
    dot = functools.partial(lax.dot_general, dimension_numbers=dims, preferred_element_type=F32)
    return dot(a[0], b[0]) + (dot(a[0], b[1]) + dot(a[1], b[0]))


def dot_full(a, b, dims):
    return lax.dot_general(a, b, dims, preferred_element_type=F32, precision=lax.Precision.HIGHEST)


def iotas():
    shape = (N, N)
    return lax.broadcasted_iota(jnp.int32, shape, 0), lax.broadcasted_iota(jnp.int32, shape, 1)


def inv_sqrt_diag(m, eye):
    picked = jnp.where(eye, m, 0.0)
    col = lax.rsqrt(jnp.sum(picked, axis=1, keepdims=True))
    row = lax.rsqrt(jnp.sum(picked, axis=0, keepdims=True))
    return col, row


def inverse_factor(m, steps):
    r, c = iotas()
    eye = r == c
    below = r > c
    one = jnp.where(eye, 1.0, 0.0)
    col, start = inv_sqrt_diag(m, eye)
    m = col * m * start
    s = jnp.where(below, m, 0.0)
    s2 = dot1(s, s, NN)
    t = one - s
    x = t + dot1(t, s2, NN)
    for _ in range(steps):
        mk = dot1(dot1(x, m, NN), x, NT)
        col, row = inv_sqrt_diag(mk, eye)
        s = jnp.where(below, col * mk * row, 0.0)
        s2 = dot1(s, s, NN)
        t = one - s
        x = col * x
        x = x - dot1(s, x, NN) + dot1(dot1(t, s2, NN), x, NN)
    x = jnp.where(r >= c, x, 0.0)
    xs = split(x)
    mk = dot3(split(dot3(xs, split(m), NN)), xs, NT)
    col, row = inv_sqrt_diag(mk, eye)
    off = jnp.where(eye, 0.0, col * mk * row)
    size = jnp.sum(off * off)
    s = jnp.where(below, off, 0.0)
    x = col * x
    step = s - dot1(s, s, NN)
    x = x - dot3(split(step), split(x), NN)
    return x * start, size


def factor_columns(m_ref, l_ref):
    r, c = iotas()

    def body(j, _):
        m = m_ref[...]
        row = jnp.sum(jnp.where(r == j, m, 0.0), axis=0, keepdims=True)
        col = jnp.sum(jnp.where(c == j, m, 0.0), axis=1, keepdims=True)
        pivot = jnp.sum(jnp.where((r == j) & (c == j), m, 0.0))
        pivot = jnp.full((1, N), pivot, F32)
        row = jnp.where(c[:1] >= j, row, 0.0)
        col = jnp.where(r[:, :1] >= j, col, 0.0)
        m_ref[...] = m - col * (row / pivot)
        l_ref[...] = jnp.where(c == j, col / jnp.sqrt(pivot), l_ref[...])
        return 0

    lax.fori_loop(0, N, body, 0)


def invert_lower(l_ref, x_ref):
    r, c = iotas()
    eye = r == c
    diag = jnp.sum(jnp.where(eye, l_ref[...], 0.0), axis=1, keepdims=True)
    x_ref[...] = jnp.where(eye, 1.0 / diag, 0.0)

    def body(k, _):
        rk, ck = r >> k, c >> k
        off = jnp.where(((rk >> 1) == (ck >> 1)) & (rk > ck), l_ref[...], 0.0)
        x = x_ref[...]
        x_ref[...] = x - dot_full(dot_full(x, off, NN), x, NN)
        return 0

    lax.fori_loop(0, 8, body, 0)


def weights_body(a, b, cross, out_ref, y_ref, z_ref, m_ref, l_ref):
    plain = a is None
    r, c = iotas()
    if plain:
        one = jnp.where(r == c, 1.0, 0.0)
        t0, t1 = one + cross.T, one + cross
        unscale = 1.0
    else:
        top = jnp.max(jnp.where(r == c, jnp.maximum(a, b), 0.0))
        top = jnp.full((1, N), top, F32)
        inv = 1.0 / top
        unscale = lax.rsqrt(top)
        a, b, cross = a * inv, b * inv, cross * inv
        sa, sb, sc = split(a), split(b), split(cross)
        t0, t1 = a + cross.T, b + cross

    def times(t0, t1):
        s0, s1 = split(t0), split(t1)
        if plain:
            left = dot1(s1[0], cross, NT) + dot1(s1[1], cross, NT)
            right = dot1(s0[0], cross, NN) + dot1(s0[1], cross, NN)
            return t0 + left, t1 + right
        left, right = dot3(s1, sc, NT), dot3(s0, sc, NN)
        return dot3(s0, sa, NN) + left, dot3(s1, sb, NN) + right

    u0, u1 = times(t0, t1)
    v0, v1 = times(u0, u1)
    us0, us1 = split(u0), split(u1)
    m = dot3(split(v0), us0, NT) + dot3(split(v1), us1, NT)
    x, size = inverse_factor(m, 1 if plain else 2)
    xs = split(x)
    out_ref[0] = (dot3(xs, us0, NN) * unscale).astype(BF16)
    out_ref[1] = (dot3(xs, us1, NN) * unscale).astype(BF16)
    good = jnp.where(size < 0.06, 1, 0)

    @pl.when(good == 0)
    def _():
        y_ref[0] = t0
        y_ref[1] = t1

        def step(it, _):
            y0, y1 = y_ref[0], y_ref[1]
            left, right = dot_full(y1, cross, NT), dot_full(y0, cross, NN)
            if plain:
                z0, z1 = y0 + left, y1 + right
            else:
                z0, z1 = dot_full(y0, a, NN) + left, dot_full(y1, b, NN) + right
            m_ref[...] = dot_full(z0, y0, NT) + dot_full(z1, y1, NT)
            z_ref[0] = jnp.where(it == 0, z0, y0)
            z_ref[1] = jnp.where(it == 0, z1, y1)
            l_ref[...] = jnp.zeros((N, N), F32)
            factor_columns(m_ref, l_ref)
            invert_lower(l_ref, m_ref)
            xi = m_ref[...]
            y_ref[0] = dot_full(xi, z_ref[0], NN)
            y_ref[1] = dot_full(xi, z_ref[1], NN)
            return 0

        lax.fori_loop(0, 2, step, 0)
        out_ref[0] = (y_ref[0] * unscale).astype(BF16)
        out_ref[1] = (y_ref[1] * unscale).astype(BF16)


def mixed(p_ref, q_ref, w_ref):
    out = dot1(p_ref[...], w_ref[0], NT) + dot1(q_ref[...], w_ref[1], NT)
    return out.astype(BF16)


def mixed_turned(p_ref, q_ref, w_ref):
    out = dot1(w_ref[0], p_ref[...], NT) + dot1(w_ref[1], q_ref[...], NT)
    return out.astype(BF16)


def send_products(turned, sides, proj_hbm, proj_ref, sems):
    copies = []
    for k, side in enumerate(sides):
        got = dot1(turned, side[...], NN).astype(BF16)
        at = pl.ds(N * k, N)
        proj_ref[:, :, N * k : N * (k + 1)] = got.reshape(VOX, ROWS, N)
        copies.append(pltpu.make_async_copy(proj_ref.at[:, :, at], proj_hbm.at[:, :, at], sems.at[k]))
        copies[-1].start()
    for copy in copies:
        copy.wait()


PARTS = jax.ShapeDtypeStruct((VOX, ROWS, 2 * N), BF16)
SENDING = [pltpu.VMEM(PARTS.shape, BF16), pltpu.SemaphoreType.DMA((2,))]
SCRATCH = [pltpu.VMEM((2, N, N), F32)] * 2 + [pltpu.VMEM((N, N), F32)] * 2
WEIGHTS = jax.ShapeDtypeStruct((2, N, N), BF16)


def full_kernel(core_ref, mine_ref, theirs_ref, p_ref, q_ref, r_ref, s_ref, *refs):
    out_ref, node_hbm, proj_hbm, a_ref, c_ref = refs[:5]
    core = core_ref[0]
    for half, ref in ((core, mine_ref), (1 - core, theirs_ref)):
        for y in range(8):
            block = 2 * y + half
            lo = pl.ds(pl.multiple_of(8 * block, 8), 8)
            hi = pl.ds(pl.multiple_of(H + 8 * block, 8), 8)
            for k in range(2):
                a_ref[k, lo, :H] = ref[y, 24 * k : 24 * k + 8, :]
                a_ref[k, hi, H:] = ref[y, 24 * k + 8 : 24 * k + 16, :]
                a_ref[k, hi, :H] = ref[y, 24 * k + 16 : 24 * k + 24, :]
            at = pl.ds(pl.multiple_of(ROWS * block, ROWS), ROWS)
            c_ref[at, :H] = ref[y, 48:64, :]
            c_ref[at, H:] = ref[y, 64:80, :]
    for k in range(2):
        a_ref[k, :H, H:] = a_ref[k, H:, :H].T
    node_ref, sem = refs[5:7]
    weights_body(a_ref[0], a_ref[1], c_ref[...], out_ref, *refs[9:])
    node_ref[...] = mixed(p_ref, q_ref, out_ref)
    copy = pltpu.make_async_copy(node_ref, node_hbm, sem)
    copy.start()
    turned = mixed_turned(p_ref, q_ref, out_ref)
    send_products(turned, (r_ref, s_ref), proj_hbm, *refs[7:9])
    copy.wait()


def full_merge(core, mine, theirs, p, q, r, s):
    return pl.pallas_call(
        full_kernel,
        out_shape=(WEIGHTS, jax.ShapeDtypeStruct(p.shape, BF16), PARTS),
        in_specs=[SMEM] + [VMEM] * 6,
        out_specs=(VMEM, HBM, HBM),
        scratch_shapes=[pltpu.VMEM((2, N, N), F32), pltpu.VMEM((N, N), F32)]
        + [pltpu.VMEM(p.shape, BF16), pltpu.SemaphoreType.DMA]
        + SENDING
        + SCRATCH,
        compiler_params=params(16),
        name="full_merge",
    )(core, mine, theirs, p, q, r, s)


def plain_kernel(cross_ref, p_hbm, q_ref, out_ref, turned_ref, p_ref, sem, *scratch):
    copy = pltpu.make_async_copy(p_hbm, p_ref, sem)
    copy.start()
    weights_body(None, None, cross_ref[...].astype(F32), out_ref, *scratch)
    copy.wait()
    turned_ref[...] = mixed_turned(p_ref, q_ref, out_ref)


def plain_merge(cross, p, q):
    return pl.pallas_call(
        plain_kernel,
        out_shape=(WEIGHTS, jax.ShapeDtypeStruct(p.shape[::-1], BF16)),
        in_specs=[VMEM, HBM, VMEM],
        out_specs=(VMEM, VMEM),
        scratch_shapes=[pltpu.VMEM(p.shape, BF16), pltpu.SemaphoreType.DMA] + SCRATCH,
        compiler_params=params(14),
        name="plain_merge",
    )(cross, p, q)


def mix_kernel(p_ref, q_ref, w_ref, out_ref):
    out_ref[...] = mixed(p_ref, q_ref, w_ref)


def mix(p, q, w):
    return pl.pallas_call(
        mix_kernel,
        out_shape=jax.ShapeDtypeStruct(p.shape, BF16),
        in_specs=[VMEM] * 3,
        out_specs=VMEM,
        compiler_params=params(6),
        name="mix",
    )(p, q, w)


def project_kernel(turned_ref, r_ref, s_ref, proj_hbm, *refs):
    send_products(turned_ref[...], (r_ref, s_ref), proj_hbm, *refs)


def project(turned, r, s):
    return pl.pallas_call(
        project_kernel,
        out_shape=PARTS,
        in_specs=[VMEM] * 3,
        out_specs=HBM,
        scratch_shapes=SENDING,
        compiler_params=params(8),
        name="project",
    )(turned, r, s)


def last_kernel(cross_ref, turned_hbm, q_ref, series_hbm, out_ref, *refs):
    turned_ref, series_ref, first_sem, second_sem, w_ref = refs[:5]
    first = pltpu.make_async_copy(turned_hbm, turned_ref, first_sem)
    first.start()
    second = pltpu.make_async_copy(series_hbm, series_ref, second_sem)
    second.start()
    weights_body(None, None, cross_ref[...].astype(F32), w_ref, *refs[5:])
    first.wait()
    second.wait()
    root = dot1(w_ref[0], turned_ref[...], NN) + dot1(w_ref[1], q_ref[...], NT)
    out_ref[...] = dot1(root, series_ref[...], NN).astype(BF16).reshape(out_ref.shape)


def last_merge(cross, turned, q, series):
    return pl.pallas_call(
        last_kernel,
        out_shape=jax.ShapeDtypeStruct((VOX, ROWS, series.shape[1]), BF16),
        in_specs=[VMEM, HBM, VMEM, HBM],
        out_specs=VMEM,
        scratch_shapes=[pltpu.VMEM(turned.shape, BF16), pltpu.VMEM(series.shape, BF16)]
        + [pltpu.SemaphoreType.DMA] * 2
        + [pltpu.VMEM((2, N, N), BF16)]
        + SCRATCH,
        compiler_params=params(16),
        name="last_merge",
    )(cross, turned, q, pltpu.with_memory_space_constraint(series, pltpu.MemorySpace.HBM))


def self_gram_kernel(p_hbm, out_ref, p_ref, sems):
    piece = p_hbm.shape[0] // 4
    copies = []
    for k in range(4):
        at = pl.ds(piece * k, piece)
        copies.append(pltpu.make_async_copy(p_hbm.at[at], p_ref.at[at], sems.at[k]))
        copies[-1].start()
    total = None
    for k in range(4):
        copies[k].wait()
        at = pl.ds(piece * k, piece)
        left, right = p_ref[at, :H], p_ref[at, H:]
        pairs = ((left, left), (right, right), (right, left))
        got = [dot1(a, b, TN) for a, b in pairs]
        total = got if total is None else [x + y for x, y in zip(total, got)]
    for k in range(3):
        out_ref[:, 8 * k : 8 * k + 8, :] = total[k].astype(BF16).reshape(VOX, 8, H)


def self_gram(p):
    return pl.pallas_call(
        self_gram_kernel,
        out_shape=jax.ShapeDtypeStruct((VOX, 24, H), BF16),
        in_specs=[HBM],
        out_specs=VMEM,
        scratch_shapes=[pltpu.VMEM(p.shape, BF16), pltpu.SemaphoreType.DMA((4,))],
        compiler_params=params(4),
        name="self_gram",
    )(pltpu.with_memory_space_constraint(p, pltpu.MemorySpace.HBM))


def cross_gram_kernel(p_ref, q_ref, out_ref):
    got = dot1(p_ref[...], q_ref[...], TN).astype(BF16)
    out_ref[:, :ROWS, :] = got[:, :H].reshape(VOX, ROWS, H)
    out_ref[:, ROWS:, :] = got[:, H:].reshape(VOX, ROWS, H)


def cross_gram(p, q):
    return pl.pallas_call(
        cross_gram_kernel,
        out_shape=jax.ShapeDtypeStruct((VOX, 2 * ROWS, H), BF16),
        in_specs=[VMEM, VMEM],
        out_specs=VMEM,
        compiler_params=params(6),
        name="cross_gram",
    )(p, q)


def rows_kernel(parts_ref, w_ref, out_ref):
    total = jnp.sum(parts_ref[...].astype(F32), axis=0)
    hi, lo = split(total)
    got = jnp.zeros((ROWS, N), F32)
    for k in range(2):
        at = slice(N * k, N * (k + 1))
        got = got + (dot1(hi[:, at], w_ref[k], NT) + dot1(lo[:, at], w_ref[k], NT))
    out_ref[...] = jnp.broadcast_to(got.astype(BF16)[None], out_ref.shape)


def cross_rows_of(parts, w):
    return pl.pallas_call(
        rows_kernel,
        out_shape=jax.ShapeDtypeStruct((VOX, ROWS, N), BF16),
        in_specs=[VMEM, VMEM],
        out_specs=VMEM,
        compiler_params=params(4),
        name="cross_rows",
    )(parts, w)


def partner(value, mask):
    return lax.ppermute(value, "grp", [(g, g ^ mask) for g in range(GRP)])


def exchange(parts):
    return lax.all_to_all(parts, "vox", 0, 0)


def same_core(rows):
    groups = [[2 * y + c for y in range(8)] for c in range(2)]
    sent = jnp.broadcast_to(rows[None], (8,) + rows.shape)
    return lax.all_to_all(sent, "vox", 0, 0, axis_index_groups=groups)


def swap_cores(value):
    return lax.ppermute(value, "vox", [(v, v ^ 1) for v in range(VOX)])


def add_up(parts):
    return jnp.sum(parts.astype(F32), axis=0)


def tree(own, series):
    core = (lax.axis_index("vox") & 1).astype(jnp.int32).reshape(1)
    other = partner(own, 1)
    own_rows = add_up(exchange(self_gram(own)))
    far_own = partner(own, 3)
    far_other = partner(other, 3)
    other_rows = partner(own_rows, 1)
    cross_rows = add_up(exchange(cross_gram(own, other)))
    rows = jnp.concatenate([own_rows, other_rows, cross_rows], axis=0)
    mine = same_core(rows)
    theirs = swap_cores(mine)
    w, left, parts = full_merge(core, mine, theirs, own, other, far_own, far_other)
    parts = exchange(parts)
    far_w = partner(w, 3)
    deep_left = partner(left, 4)
    deep_right = partner(left, 7)
    cross = exchange(cross_rows_of(parts, far_w))
    right = mix(far_own, far_other, far_w)
    w, turned = plain_merge(cross.reshape(N, N), left, right)

    parts = project(turned, deep_left, deep_right)
    parts = exchange(parts)
    deep_w = partner(w, 4)
    cross = exchange(cross_rows_of(parts, deep_w))
    right = mix(deep_left, deep_right, deep_w)
    parts = last_merge(cross.reshape(N, N), turned, right, series)
    return add_up(exchange(parts))


def local(group_basis, timeseries):
    return tree(group_basis[0], timeseries[0])[None]


def solution(mesh):
    return jax.shard_map(
        local,
        mesh=mesh,
        in_specs=(P("grp", "vox", None), P("grp", "vox", None)),
        out_specs=P("grp", "vox", None),
        check_vma=False,
    )
```

```python
import functools

import jax
import jax.numpy as jnp
from jax import lax
from jax.experimental import pallas as pl
from jax.experimental.pallas import tpu as pltpu
from jax.sharding import PartitionSpec as P


N = 256
H = 128
VOX = 16
GRP = 32
ROWS = N // VOX
F32 = jnp.float32
BF16 = jnp.bfloat16

NN = (((1,), (0,)), ((), ()))
NT = (((1,), (1,)), ((), ()))
VMEM = pl.BlockSpec(memory_space=pltpu.VMEM)
SMEM = pl.BlockSpec(memory_space=pltpu.SMEM)
HBM = pl.BlockSpec(memory_space=pltpu.MemorySpace.HBM)


def params(mib):
    return pltpu.CompilerParams(vmem_limit_bytes=mib << 20)


def dot1(a, b, dims):
    return lax.dot_general(a.astype(BF16), b.astype(BF16), dims, preferred_element_type=F32)


def split(x):
    hi = x.astype(BF16)
    return hi, (x - hi.astype(F32)).astype(BF16)


def dot3(a, b, dims):
    dot = functools.partial(lax.dot_general, dimension_numbers=dims, preferred_element_type=F32)
    return dot(a[0], b[0]) + (dot(a[0], b[1]) + dot(a[1], b[0]))


def dot_full(a, b, dims):
    return lax.dot_general(a, b, dims, preferred_element_type=F32, precision=lax.Precision.HIGHEST)


def iotas():
    shape = (N, N)
    return lax.broadcasted_iota(jnp.int32, shape, 0), lax.broadcasted_iota(jnp.int32, shape, 1)


def inv_sqrt_diag(m, eye):
    picked = jnp.where(eye, m, 0.0)
    col = lax.rsqrt(jnp.sum(picked, axis=1, keepdims=True))
    row = lax.rsqrt(jnp.sum(picked, axis=0, keepdims=True))
    return col, row


def inverse_factor(m, steps):
    r, c = iotas()
    eye = r == c
    below = r > c
    one = jnp.where(eye, 1.0, 0.0)
    col, start = inv_sqrt_diag(m, eye)
    m = col * m * start
    s = jnp.where(below, m, 0.0)
    s2 = dot1(s, s, NN)
    t = one - s
    x = t + dot1(t, s2, NN)
    for _ in range(steps):
        mk = dot1(dot1(x, m, NN), x, NT)
        col, row = inv_sqrt_diag(mk, eye)
        s = jnp.where(below, col * mk * row, 0.0)
        s2 = dot1(s, s, NN)
        t = one - s
        x = col * x
        x = x - dot1(s, x, NN) + dot1(dot1(t, s2, NN), x, NN)
    x = jnp.where(r >= c, x, 0.0)
    xs = split(x)
    mk = dot3(split(dot3(xs, split(m), NN)), xs, NT)
    col, row = inv_sqrt_diag(mk, eye)
    off = jnp.where(eye, 0.0, col * mk * row)
    size = jnp.sum(off * off)
    s = jnp.where(below, off, 0.0)
    x = col * x
    step = s - dot1(s, s, NN)
    x = x - dot3(split(step), split(x), NN)
    return x * start, size


def factor_columns(m_ref, l_ref):
    r, c = iotas()

    def body(j, _):
        m = m_ref[...]
        row = jnp.sum(jnp.where(r == j, m, 0.0), axis=0, keepdims=True)
        col = jnp.sum(jnp.where(c == j, m, 0.0), axis=1, keepdims=True)
        pivot = jnp.sum(jnp.where((r == j) & (c == j), m, 0.0))
        pivot = jnp.full((1, N), pivot, F32)
        row = jnp.where(c[:1] >= j, row, 0.0)
        col = jnp.where(r[:, :1] >= j, col, 0.0)
        m_ref[...] = m - col * (row / pivot)
        l_ref[...] = jnp.where(c == j, col / jnp.sqrt(pivot), l_ref[...])
        return 0

    lax.fori_loop(0, N, body, 0)


def invert_lower(l_ref, x_ref):
    r, c = iotas()
    eye = r == c
    diag = jnp.sum(jnp.where(eye, l_ref[...], 0.0), axis=1, keepdims=True)
    x_ref[...] = jnp.where(eye, 1.0 / diag, 0.0)

    def body(k, _):
        rk, ck = r >> k, c >> k
        off = jnp.where(((rk >> 1) == (ck >> 1)) & (rk > ck), l_ref[...], 0.0)
        x = x_ref[...]
        x_ref[...] = x - dot_full(dot_full(x, off, NN), x, NN)
        return 0

    lax.fori_loop(0, 8, body, 0)


def weights_body(a, b, cross, out_ref, y_ref, z_ref, m_ref, l_ref):
    plain = a is None
    r, c = iotas()
    if plain:
        one = jnp.where(r == c, 1.0, 0.0)
        t0, t1 = one + cross.T, one + cross
        unscale = 1.0
    else:
        top = jnp.max(jnp.where(r == c, jnp.maximum(a, b), 0.0))
        top = jnp.full((1, N), top, F32)
        inv = 1.0 / top
        unscale = lax.rsqrt(top)
        a, b, cross = a * inv, b * inv, cross * inv
        sa, sb, sc = split(a), split(b), split(cross)
        t0, t1 = a + cross.T, b + cross

    def times(t0, t1):
        s0, s1 = split(t0), split(t1)
        if plain:
            left = dot1(s1[0], cross, NT) + dot1(s1[1], cross, NT)
            right = dot1(s0[0], cross, NN) + dot1(s0[1], cross, NN)
            return t0 + left, t1 + right
        left, right = dot3(s1, sc, NT), dot3(s0, sc, NN)
        return dot3(s0, sa, NN) + left, dot3(s1, sb, NN) + right

    u0, u1 = times(t0, t1)
    v0, v1 = times(u0, u1)
    us0, us1 = split(u0), split(u1)
    m = dot3(split(v0), us0, NT) + dot3(split(v1), us1, NT)
    x, size = inverse_factor(m, 1 if plain else 2)
    xs = split(x)
    out_ref[0] = (dot3(xs, us0, NN) * unscale).astype(BF16)
    out_ref[1] = (dot3(xs, us1, NN) * unscale).astype(BF16)
    good = jnp.where(size < 0.06, 1, 0)

    @pl.when(good == 0)
    def _():
        y_ref[0] = t0
        y_ref[1] = t1

        def step(it, _):
            y0, y1 = y_ref[0], y_ref[1]
            left, right = dot_full(y1, cross, NT), dot_full(y0, cross, NN)
            if plain:
                z0, z1 = y0 + left, y1 + right
            else:
                z0, z1 = dot_full(y0, a, NN) + left, dot_full(y1, b, NN) + right
            m_ref[...] = dot_full(z0, y0, NT) + dot_full(z1, y1, NT)
            z_ref[0] = jnp.where(it == 0, z0, y0)
            z_ref[1] = jnp.where(it == 0, z1, y1)
            l_ref[...] = jnp.zeros((N, N), F32)
            factor_columns(m_ref, l_ref)
            invert_lower(l_ref, m_ref)
            xi = m_ref[...]
            y_ref[0] = dot_full(xi, z_ref[0], NN)
            y_ref[1] = dot_full(xi, z_ref[1], NN)
            return 0

        lax.fori_loop(0, 2, step, 0)
        out_ref[0] = (y_ref[0] * unscale).astype(BF16)
        out_ref[1] = (y_ref[1] * unscale).astype(BF16)


def mixed(p_ref, q_ref, w_ref):
    out = dot1(p_ref[...], w_ref[0], NT) + dot1(q_ref[...], w_ref[1], NT)
    return out.astype(BF16)


def mixed_turned(p_ref, q_ref, w_ref):
    out = dot1(w_ref[0], p_ref[...], NT) + dot1(w_ref[1], q_ref[...], NT)
    return out.astype(BF16)


def send_products(turned, sides, proj_hbm, proj_ref, sems):
    copies = []
    for k, side in enumerate(sides):
        got = dot1(turned, side[...], NN).astype(BF16)
        at = pl.ds(N * k, N)
        proj_ref[:, :, N * k : N * (k + 1)] = got.reshape(VOX, ROWS, N)
        copies.append(pltpu.make_async_copy(proj_ref.at[:, :, at], proj_hbm.at[:, :, at], sems.at[k]))
        copies[-1].start()
    for copy in copies:
        copy.wait()


PARTS = jax.ShapeDtypeStruct((VOX, ROWS, 2 * N), BF16)
SENDING = [pltpu.VMEM(PARTS.shape, BF16), pltpu.SemaphoreType.DMA((2,))]
SCRATCH = [pltpu.VMEM((2, N, N), F32)] * 2 + [pltpu.VMEM((N, N), F32)] * 2
WEIGHTS = jax.ShapeDtypeStruct((2, N, N), BF16)


def full_kernel(core_ref, mine_ref, theirs_ref, p_ref, q_ref, r_ref, s_ref, *refs):
    out_ref, node_hbm, proj_hbm, a_ref, c_ref = refs[:5]
    core = core_ref[0]
    for half, ref in ((core, mine_ref), (1 - core, theirs_ref)):
        for y in range(8):
            block = 2 * y + half
            lo = pl.ds(pl.multiple_of(8 * block, 8), 8)
            hi = pl.ds(pl.multiple_of(H + 8 * block, 8), 8)
            for k in range(2):
                a_ref[k, lo, :H] = ref[y, 24 * k : 24 * k + 8, :]
                a_ref[k, hi, H:] = ref[y, 24 * k + 8 : 24 * k + 16, :]
                a_ref[k, hi, :H] = ref[y, 24 * k + 16 : 24 * k + 24, :]
            at = pl.ds(pl.multiple_of(ROWS * block, ROWS), ROWS)
            c_ref[at, :H] = ref[y, 48:64, :]
            c_ref[at, H:] = ref[y, 64:80, :]
    for k in range(2):
        a_ref[k, :H, H:] = a_ref[k, H:, :H].T
    node_ref, sem = refs[5:7]
    weights_body(a_ref[0], a_ref[1], c_ref[...], out_ref, *refs[9:])
    node_ref[...] = mixed(p_ref, q_ref, out_ref)
    copy = pltpu.make_async_copy(node_ref, node_hbm, sem)
    copy.start()
    turned = mixed_turned(p_ref, q_ref, out_ref)
    send_products(turned, (r_ref, s_ref), proj_hbm, *refs[7:9])
    copy.wait()


def full_merge(core, mine, theirs, p, q, r, s):
    return pl.pallas_call(
        full_kernel,
        out_shape=(WEIGHTS, jax.ShapeDtypeStruct(p.shape, BF16), PARTS),
        in_specs=[SMEM] + [VMEM] * 6,
        out_specs=(VMEM, HBM, HBM),
        scratch_shapes=[pltpu.VMEM((2, N, N), F32), pltpu.VMEM((N, N), F32)]
        + [pltpu.VMEM(p.shape, BF16), pltpu.SemaphoreType.DMA]
        + SENDING
        + SCRATCH,
        compiler_params=params(16),
        name="full_merge",
    )(core, mine, theirs, p, q, r, s)


def plain_kernel(cross_ref, p_hbm, q_ref, out_ref, turned_ref, p_ref, sem, *scratch):
    copy = pltpu.make_async_copy(p_hbm, p_ref, sem)
    copy.start()
    weights_body(None, None, cross_ref[...].astype(F32), out_ref, *scratch)
    copy.wait()
    turned_ref[...] = mixed_turned(p_ref, q_ref, out_ref)


def plain_merge(cross, p, q):
    return pl.pallas_call(
        plain_kernel,
        out_shape=(WEIGHTS, jax.ShapeDtypeStruct(p.shape[::-1], BF16)),
        in_specs=[VMEM, HBM, VMEM],
        out_specs=(VMEM, VMEM),
        scratch_shapes=[pltpu.VMEM(p.shape, BF16), pltpu.SemaphoreType.DMA] + SCRATCH,
        compiler_params=params(14),
        name="plain_merge",
    )(cross, p, q)


def mix_kernel(p_ref, q_ref, w_ref, out_ref):
    out_ref[...] = mixed(p_ref, q_ref, w_ref)


def mix(p, q, w):
    return pl.pallas_call(
        mix_kernel,
        out_shape=jax.ShapeDtypeStruct(p.shape, BF16),
        in_specs=[VMEM] * 3,
        out_specs=VMEM,
        compiler_params=params(6),
        name="mix",
    )(p, q, w)


def project_kernel(turned_ref, r_ref, s_ref, proj_hbm, *refs):
    send_products(turned_ref[...], (r_ref, s_ref), proj_hbm, *refs)


def project(turned, r, s):
    return pl.pallas_call(
        project_kernel,
        out_shape=PARTS,
        in_specs=[VMEM] * 3,
        out_specs=HBM,
        scratch_shapes=SENDING,
        compiler_params=params(8),
        name="project",
    )(turned, r, s)


def last_kernel(cross_ref, turned_hbm, q_ref, series_hbm, out_ref, *refs):
    turned_ref, series_ref, first_sem, second_sem, w_ref = refs[:5]
    first = pltpu.make_async_copy(turned_hbm, turned_ref, first_sem)
    first.start()
    second = pltpu.make_async_copy(series_hbm, series_ref, second_sem)
    second.start()
    weights_body(None, None, cross_ref[...].astype(F32), w_ref, *refs[5:])
    first.wait()
    second.wait()
    root = dot1(w_ref[0], turned_ref[...], NN) + dot1(w_ref[1], q_ref[...], NT)
    out_ref[...] = dot1(root, series_ref[...], NN).astype(BF16).reshape(out_ref.shape)


def last_merge(cross, turned, q, series):
    return pl.pallas_call(
        last_kernel,
        out_shape=jax.ShapeDtypeStruct((VOX, ROWS, series.shape[1]), BF16),
        in_specs=[VMEM, HBM, VMEM, HBM],
        out_specs=VMEM,
        scratch_shapes=[pltpu.VMEM(turned.shape, BF16), pltpu.VMEM(series.shape, BF16)]
        + [pltpu.SemaphoreType.DMA] * 2
        + [pltpu.VMEM((2, N, N), BF16)]
        + SCRATCH,
        compiler_params=params(16),
        name="last_merge",
    )(cross, turned, q, pltpu.with_memory_space_constraint(series, pltpu.MemorySpace.HBM))


def lower_blocks(p, q):
    pairs = ((0, 0), (1, 1), (1, 0))
    half = lambda k: slice(H * k, H * (k + 1))
    return [dot1(p[half(i), :], q[:, half(j)], NN) for i, j in pairs]


def self_gram_kernel(p_hbm, turned_ref, out_ref, p_ref, sem):
    copy = pltpu.make_async_copy(p_hbm, p_ref, sem)
    copy.start()
    copy.wait()
    p = p_ref[...]
    turned = p.T
    turned_ref[...] = turned
    for k, block in enumerate(lower_blocks(turned, p)):
        out_ref[:, 8 * k : 8 * k + 8, :] = block.astype(BF16).reshape(VOX, 8, H)


def self_gram(p):
    return pl.pallas_call(
        self_gram_kernel,
        out_shape=(
            jax.ShapeDtypeStruct(p.shape[::-1], BF16),
            jax.ShapeDtypeStruct((VOX, 24, H), BF16),
        ),
        in_specs=[HBM],
        out_specs=(VMEM, VMEM),
        scratch_shapes=[pltpu.VMEM(p.shape, BF16), pltpu.SemaphoreType.DMA],
        compiler_params=params(6),
        name="self_gram",
    )(pltpu.with_memory_space_constraint(p, pltpu.MemorySpace.HBM))


def pair_gram_kernel(turned_ref, q_ref, own_ref, out_ref):
    q = q_ref[...]
    out_ref[:, :24, :] = own_ref[...]
    for k, block in enumerate(lower_blocks(q.T, q)):
        out_ref[:, 24 + 8 * k : 32 + 8 * k, :] = block.astype(BF16).reshape(VOX, 8, H)
    for k in range(2):
        got = dot1(turned_ref[...], q[:, H * k : H * (k + 1)], NN).astype(BF16)
        out_ref[:, 48 + ROWS * k : 64 + ROWS * k, :] = got.reshape(VOX, ROWS, H)


def pair_gram(turned, q, own):
    return pl.pallas_call(
        pair_gram_kernel,
        out_shape=jax.ShapeDtypeStruct((VOX, 80, H), BF16),
        in_specs=[VMEM] * 3,
        out_specs=VMEM,
        compiler_params=params(8),
        name="pair_gram",
    )(turned, q, own)


def rows_kernel(parts_ref, w_ref, out_ref):
    total = jnp.sum(parts_ref[...].astype(F32), axis=0)
    hi, lo = split(total)
    got = jnp.zeros((ROWS, N), F32)
    for k in range(2):
        at = slice(N * k, N * (k + 1))
        got = got + (dot1(hi[:, at], w_ref[k], NT) + dot1(lo[:, at], w_ref[k], NT))
    out_ref[...] = jnp.broadcast_to(got.astype(BF16)[None], out_ref.shape)


def cross_rows_of(parts, w):
    return pl.pallas_call(
        rows_kernel,
        out_shape=jax.ShapeDtypeStruct((VOX, ROWS, N), BF16),
        in_specs=[VMEM, VMEM],
        out_specs=VMEM,
        compiler_params=params(4),
        name="cross_rows",
    )(parts, w)


def partner(value, mask):
    return lax.ppermute(value, "grp", [(g, g ^ mask) for g in range(GRP)])


def exchange(parts):
    return lax.all_to_all(parts, "vox", 0, 0)


def same_core(rows):
    groups = [[2 * y + c for y in range(8)] for c in range(2)]
    sent = jnp.broadcast_to(rows[None], (8,) + rows.shape)
    return lax.all_to_all(sent, "vox", 0, 0, axis_index_groups=groups)


def swap_cores(value):
    return lax.ppermute(value, "vox", [(v, v ^ 1) for v in range(VOX)])


def add_up(parts):
    return jnp.sum(parts.astype(F32), axis=0)


def tree(own, series):
    core = (lax.axis_index("vox") & 1).astype(jnp.int32).reshape(1)
    other = partner(own, 1)
    turned, own_parts = self_gram(own)
    far_own = partner(own, 3)
    far_other = partner(other, 3)
    parts = pair_gram(turned, other, own_parts)
    rows = add_up(exchange(parts))
    mine = same_core(rows)
    theirs = swap_cores(mine)
    w, left, parts = full_merge(core, mine, theirs, own, other, far_own, far_other)
    parts = exchange(parts)
    far_w = partner(w, 3)
    deep_left = partner(left, 4)
    deep_right = partner(left, 7)
    cross = exchange(cross_rows_of(parts, far_w))
    right = mix(far_own, far_other, far_w)
    w, turned = plain_merge(cross.reshape(N, N), left, right)

    parts = project(turned, deep_left, deep_right)
    parts = exchange(parts)
    deep_w = partner(w, 4)
    cross = exchange(cross_rows_of(parts, deep_w))
    right = mix(deep_left, deep_right, deep_w)
    parts = last_merge(cross.reshape(N, N), turned, right, series)
    return add_up(exchange(parts))


def local(group_basis, timeseries):
    return tree(group_basis[0], timeseries[0])[None]


def solution(mesh):
    return jax.shard_map(
        local,
        mesh=mesh,
        in_specs=(P("grp", "vox", None), P("grp", "vox", None)),
        out_specs=P("grp", "vox", None),
        check_vma=False,
    )
```

```python
import functools

import jax
import jax.numpy as jnp
from jax import lax
from jax.experimental import pallas as pl
from jax.experimental.pallas import tpu as pltpu
from jax.sharding import PartitionSpec as P


N = 256
H = 128
VOX = 16
GRP = 32
ROWS = N // VOX
F32 = jnp.float32
BF16 = jnp.bfloat16

NN = (((1,), (0,)), ((), ()))
NT = (((1,), (1,)), ((), ()))
VMEM = pl.BlockSpec(memory_space=pltpu.VMEM)
SMEM = pl.BlockSpec(memory_space=pltpu.SMEM)
HBM = pl.BlockSpec(memory_space=pltpu.MemorySpace.HBM)


def params(mib):
    return pltpu.CompilerParams(vmem_limit_bytes=mib << 20)


def dot1(a, b, dims):
    return lax.dot_general(a.astype(BF16), b.astype(BF16), dims, preferred_element_type=F32)


def split(x):
    hi = x.astype(BF16)
    return hi, (x - hi.astype(F32)).astype(BF16)


def dot3(a, b, dims):
    dot = functools.partial(lax.dot_general, dimension_numbers=dims, preferred_element_type=F32)
    return dot(a[0], b[0]) + (dot(a[0], b[1]) + dot(a[1], b[0]))


def dot_full(a, b, dims):
    return lax.dot_general(a, b, dims, preferred_element_type=F32, precision=lax.Precision.HIGHEST)


def iotas():
    shape = (N, N)
    return lax.broadcasted_iota(jnp.int32, shape, 0), lax.broadcasted_iota(jnp.int32, shape, 1)


def inv_sqrt_diag(m, eye):
    picked = jnp.where(eye, m, 0.0)
    col = lax.rsqrt(jnp.sum(picked, axis=1, keepdims=True))
    row = lax.rsqrt(jnp.sum(picked, axis=0, keepdims=True))
    return col, row


def inverse_factor(m, steps):
    r, c = iotas()
    eye = r == c
    below = r > c
    one = jnp.where(eye, 1.0, 0.0)
    col, start = inv_sqrt_diag(m, eye)
    m = col * m * start
    s = jnp.where(below, m, 0.0)
    s2 = dot1(s, s, NN)
    t = one - s
    x = t + dot1(t, s2, NN)
    for _ in range(steps):
        mk = dot1(dot1(x, m, NN), x, NT)
        col, row = inv_sqrt_diag(mk, eye)
        s = jnp.where(below, col * mk * row, 0.0)
        s2 = dot1(s, s, NN)
        t = one - s
        x = col * x
        x = x - dot1(s, x, NN) + dot1(dot1(t, s2, NN), x, NN)
    x = jnp.where(r >= c, x, 0.0)
    xs = split(x)
    mk = dot3(split(dot3(xs, split(m), NN)), xs, NT)
    col, row = inv_sqrt_diag(mk, eye)
    off = jnp.where(eye, 0.0, col * mk * row)
    size = jnp.sum(off * off)
    s = jnp.where(below, off, 0.0)
    x = col * x
    step = s - dot1(s, s, NN)
    x = x - dot3(split(step), split(x), NN)
    return x * start, size


def factor_columns(m_ref, l_ref):
    r, c = iotas()

    def body(j, _):
        m = m_ref[...]
        row = jnp.sum(jnp.where(r == j, m, 0.0), axis=0, keepdims=True)
        col = jnp.sum(jnp.where(c == j, m, 0.0), axis=1, keepdims=True)
        pivot = jnp.sum(jnp.where((r == j) & (c == j), m, 0.0))
        pivot = jnp.full((1, N), pivot, F32)
        row = jnp.where(c[:1] >= j, row, 0.0)
        col = jnp.where(r[:, :1] >= j, col, 0.0)
        m_ref[...] = m - col * (row / pivot)
        l_ref[...] = jnp.where(c == j, col / jnp.sqrt(pivot), l_ref[...])
        return 0

    lax.fori_loop(0, N, body, 0)


def invert_lower(l_ref, x_ref):
    r, c = iotas()
    eye = r == c
    diag = jnp.sum(jnp.where(eye, l_ref[...], 0.0), axis=1, keepdims=True)
    x_ref[...] = jnp.where(eye, 1.0 / diag, 0.0)

    def body(k, _):
        rk, ck = r >> k, c >> k
        off = jnp.where(((rk >> 1) == (ck >> 1)) & (rk > ck), l_ref[...], 0.0)
        x = x_ref[...]
        x_ref[...] = x - dot_full(dot_full(x, off, NN), x, NN)
        return 0

    lax.fori_loop(0, 8, body, 0)


def weights_body(a, b, cross, out_ref, y_ref, z_ref, m_ref, l_ref):
    plain = a is None
    r, c = iotas()
    if plain:
        one = jnp.where(r == c, 1.0, 0.0)
        t0, t1 = one + cross.T, one + cross
        unscale = 1.0
    else:
        top = jnp.max(jnp.where(r == c, jnp.maximum(a, b), 0.0))
        top = jnp.full((1, N), top, F32)
        inv = 1.0 / top
        unscale = lax.rsqrt(top)
        a, b, cross = a * inv, b * inv, cross * inv
        sa, sb, sc = split(a), split(b), split(cross)
        t0, t1 = a + cross.T, b + cross

    def times(t0, t1):
        s0, s1 = split(t0), split(t1)
        if plain:
            left = dot1(s1[0], cross, NT) + dot1(s1[1], cross, NT)
            right = dot1(s0[0], cross, NN) + dot1(s0[1], cross, NN)
            return t0 + left, t1 + right
        left, right = dot3(s1, sc, NT), dot3(s0, sc, NN)
        return dot3(s0, sa, NN) + left, dot3(s1, sb, NN) + right

    u0, u1 = times(t0, t1)
    v0, v1 = times(u0, u1)
    us0, us1 = split(u0), split(u1)
    m = dot3(split(v0), us0, NT) + dot3(split(v1), us1, NT)
    x, size = inverse_factor(m, 1 if plain else 2)
    xs = split(x)
    out_ref[0] = (dot3(xs, us0, NN) * unscale).astype(BF16)
    out_ref[1] = (dot3(xs, us1, NN) * unscale).astype(BF16)
    good = jnp.where(size < 0.06, 1, 0)

    @pl.when(good == 0)
    def _():
        y_ref[0] = t0
        y_ref[1] = t1

        def step(it, _):
            y0, y1 = y_ref[0], y_ref[1]
            left, right = dot_full(y1, cross, NT), dot_full(y0, cross, NN)
            if plain:
                z0, z1 = y0 + left, y1 + right
            else:
                z0, z1 = dot_full(y0, a, NN) + left, dot_full(y1, b, NN) + right
            m_ref[...] = dot_full(z0, y0, NT) + dot_full(z1, y1, NT)
            z_ref[0] = jnp.where(it == 0, z0, y0)
            z_ref[1] = jnp.where(it == 0, z1, y1)
            l_ref[...] = jnp.zeros((N, N), F32)
            factor_columns(m_ref, l_ref)
            invert_lower(l_ref, m_ref)
            xi = m_ref[...]
            y_ref[0] = dot_full(xi, z_ref[0], NN)
            y_ref[1] = dot_full(xi, z_ref[1], NN)
            return 0

        lax.fori_loop(0, 2, step, 0)
        out_ref[0] = (y_ref[0] * unscale).astype(BF16)
        out_ref[1] = (y_ref[1] * unscale).astype(BF16)


def mixed(p_ref, q_ref, w_ref):
    out = dot1(p_ref[...], w_ref[0], NT) + dot1(q_ref[...], w_ref[1], NT)
    return out.astype(BF16)


def mixed_turned(p_ref, q_ref, w_ref):
    out = dot1(w_ref[0], p_ref[...], NT) + dot1(w_ref[1], q_ref[...], NT)
    return out.astype(BF16)


def send_products(turned, sides, proj_hbm, proj_ref, sems):
    copies = []
    for k, side in enumerate(sides):
        got = dot1(turned, side[...], NN).astype(BF16)
        at = pl.ds(N * k, N)
        proj_ref[:, :, N * k : N * (k + 1)] = got.reshape(VOX, ROWS, N)
        copies.append(pltpu.make_async_copy(proj_ref.at[:, :, at], proj_hbm.at[:, :, at], sems.at[k]))
        copies[-1].start()
    for copy in copies:
        copy.wait()


PARTS = jax.ShapeDtypeStruct((VOX, ROWS, 2 * N), BF16)
SENDING = [pltpu.VMEM(PARTS.shape, BF16), pltpu.SemaphoreType.DMA((2,))]
SCRATCH = [pltpu.VMEM((2, N, N), F32)] * 2 + [pltpu.VMEM((N, N), F32)] * 2
WEIGHTS = jax.ShapeDtypeStruct((2, N, N), BF16)


def full_kernel(core_ref, mine_ref, theirs_ref, p_ref, q_ref, r_ref, s_ref, *refs):
    out_ref, node_hbm, proj_hbm, a_ref, c_ref = refs[:5]
    core = core_ref[0]
    for half, ref in ((core, mine_ref), (1 - core, theirs_ref)):
        for y in range(8):
            block = 2 * y + half
            lo = pl.ds(pl.multiple_of(8 * block, 8), 8)
            hi = pl.ds(pl.multiple_of(H + 8 * block, 8), 8)
            for k in range(2):
                a_ref[k, lo, :H] = ref[y, 24 * k : 24 * k + 8, :]
                a_ref[k, hi, H:] = ref[y, 24 * k + 8 : 24 * k + 16, :]
                a_ref[k, hi, :H] = ref[y, 24 * k + 16 : 24 * k + 24, :]
            at = pl.ds(pl.multiple_of(ROWS * block, ROWS), ROWS)
            c_ref[at, :H] = ref[y, 48:64, :]
            c_ref[at, H:] = ref[y, 64:80, :]
    for k in range(2):
        a_ref[k, :H, H:] = a_ref[k, H:, :H].T
    node_ref, sem = refs[5:7]
    weights_body(a_ref[0], a_ref[1], c_ref[...], out_ref, *refs[9:])
    node_ref[...] = mixed(p_ref, q_ref, out_ref)
    copy = pltpu.make_async_copy(node_ref, node_hbm, sem)
    copy.start()
    turned = mixed_turned(p_ref, q_ref, out_ref)
    send_products(turned, (r_ref, s_ref), proj_hbm, *refs[7:9])
    copy.wait()


def full_merge(core, mine, theirs, p, q, r, s):
    return pl.pallas_call(
        full_kernel,
        out_shape=(WEIGHTS, jax.ShapeDtypeStruct(p.shape, BF16), PARTS),
        in_specs=[SMEM] + [VMEM] * 6,
        out_specs=(VMEM, HBM, HBM),
        scratch_shapes=[pltpu.VMEM((2, N, N), F32), pltpu.VMEM((N, N), F32)]
        + [pltpu.VMEM(p.shape, BF16), pltpu.SemaphoreType.DMA]
        + SENDING
        + SCRATCH,
        compiler_params=params(16),
        name="full_merge",
    )(core, mine, theirs, p, q, r, s)


def plain_kernel(cross_ref, p_hbm, q_ref, out_ref, turned_ref, p_ref, sem, *scratch):
    copy = pltpu.make_async_copy(p_hbm, p_ref, sem)
    copy.start()
    weights_body(None, None, cross_ref[...].astype(F32), out_ref, *scratch)
    copy.wait()
    turned_ref[...] = mixed_turned(p_ref, q_ref, out_ref)


def plain_merge(cross, p, q):
    return pl.pallas_call(
        plain_kernel,
        out_shape=(WEIGHTS, jax.ShapeDtypeStruct(p.shape[::-1], BF16)),
        in_specs=[VMEM, HBM, VMEM],
        out_specs=(VMEM, VMEM),
        scratch_shapes=[pltpu.VMEM(p.shape, BF16), pltpu.SemaphoreType.DMA] + SCRATCH,
        compiler_params=params(14),
        name="plain_merge",
    )(cross, p, q)


def mix_kernel(p_ref, q_ref, w_ref, out_ref):
    out_ref[...] = mixed(p_ref, q_ref, w_ref)


def mix(p, q, w):
    return pl.pallas_call(
        mix_kernel,
        out_shape=jax.ShapeDtypeStruct(p.shape, BF16),
        in_specs=[VMEM] * 3,
        out_specs=VMEM,
        compiler_params=params(6),
        name="mix",
    )(p, q, w)


def project_kernel(turned_ref, r_ref, s_ref, proj_hbm, *refs):
    send_products(turned_ref[...], (r_ref, s_ref), proj_hbm, *refs)


def project(turned, r, s):
    return pl.pallas_call(
        project_kernel,
        out_shape=PARTS,
        in_specs=[VMEM] * 3,
        out_specs=HBM,
        scratch_shapes=SENDING,
        compiler_params=params(8),
        name="project",
    )(turned, r, s)


def last_kernel(cross_ref, turned_hbm, q_ref, series_hbm, out_ref, *refs):
    turned_ref, series_ref, first_sem, second_sem, w_ref = refs[:5]
    first = pltpu.make_async_copy(turned_hbm, turned_ref, first_sem)
    first.start()
    second = pltpu.make_async_copy(series_hbm, series_ref, second_sem)
    second.start()
    weights_body(None, None, cross_ref[...].astype(F32), w_ref, *refs[5:])
    first.wait()
    second.wait()
    root = dot1(w_ref[0], turned_ref[...], NN) + dot1(w_ref[1], q_ref[...], NT)
    out_ref[...] = dot1(root, series_ref[...], NN).astype(BF16).reshape(out_ref.shape)


def last_merge(cross, turned, q, series):
    return pl.pallas_call(
        last_kernel,
        out_shape=jax.ShapeDtypeStruct((VOX, ROWS, series.shape[1]), BF16),
        in_specs=[VMEM, HBM, VMEM, HBM],
        out_specs=VMEM,
        scratch_shapes=[pltpu.VMEM(turned.shape, BF16), pltpu.VMEM(series.shape, BF16)]
        + [pltpu.SemaphoreType.DMA] * 2
        + [pltpu.VMEM((2, N, N), BF16)]
        + SCRATCH,
        compiler_params=params(16),
        name="last_merge",
    )(cross, turned, q, pltpu.with_memory_space_constraint(series, pltpu.MemorySpace.HBM))


def lower_blocks(p, q):
    pairs = ((0, 0), (1, 1), (1, 0))
    half = lambda k: slice(H * k, H * (k + 1))
    return [dot1(p[half(i), :], q[:, half(j)], NN) for i, j in pairs]


def self_gram_kernel(p_hbm, turned_ref, out_ref, p_ref, sem):
    copy = pltpu.make_async_copy(p_hbm, p_ref, sem)
    copy.start()
    copy.wait()
    p = p_ref[...]
    turned = p.T
    turned_ref[...] = turned
    for k, block in enumerate(lower_blocks(turned, p)):
        out_ref[:, 8 * k : 8 * k + 8, :] = block.astype(BF16).reshape(VOX, 8, H)


def self_gram(p):
    return pl.pallas_call(
        self_gram_kernel,
        out_shape=(
            jax.ShapeDtypeStruct(p.shape[::-1], BF16),
            jax.ShapeDtypeStruct((VOX, 24, H), BF16),
        ),
        in_specs=[HBM],
        out_specs=(VMEM, VMEM),
        scratch_shapes=[pltpu.VMEM(p.shape, BF16), pltpu.SemaphoreType.DMA],
        compiler_params=params(6),
        name="self_gram",
    )(pltpu.with_memory_space_constraint(p, pltpu.MemorySpace.HBM))


def cross_gram_kernel(turned_ref, q_ref, out_ref):
    for k in range(2):
        got = dot1(turned_ref[...], q_ref[:, H * k : H * (k + 1)], NN).astype(BF16)
        out_ref[:, ROWS * k : ROWS * (k + 1), :] = got.reshape(VOX, ROWS, H)


def cross_gram(turned, q):
    return pl.pallas_call(
        cross_gram_kernel,
        out_shape=jax.ShapeDtypeStruct((VOX, 2 * ROWS, H), BF16),
        in_specs=[VMEM] * 2,
        out_specs=VMEM,
        compiler_params=params(6),
        name="cross_gram",
    )(turned, q)


def rows_kernel(parts_ref, w_ref, out_ref):
    total = jnp.sum(parts_ref[...].astype(F32), axis=0)
    hi, lo = split(total)
    got = jnp.zeros((ROWS, N), F32)
    for k in range(2):
        at = slice(N * k, N * (k + 1))
        got = got + (dot1(hi[:, at], w_ref[k], NT) + dot1(lo[:, at], w_ref[k], NT))
    out_ref[...] = jnp.broadcast_to(got.astype(BF16)[None], out_ref.shape)


def cross_rows_of(parts, w):
    return pl.pallas_call(
        rows_kernel,
        out_shape=jax.ShapeDtypeStruct((VOX, ROWS, N), BF16),
        in_specs=[VMEM, VMEM],
        out_specs=VMEM,
        compiler_params=params(4),
        name="cross_rows",
    )(parts, w)


def partner(value, mask):
    return lax.ppermute(value, "grp", [(g, g ^ mask) for g in range(GRP)])


def exchange(parts):
    return lax.all_to_all(parts, "vox", 0, 0)


def same_core(rows):
    groups = [[2 * y + c for y in range(8)] for c in range(2)]
    sent = jnp.broadcast_to(rows[None], (8,) + rows.shape)
    return lax.all_to_all(sent, "vox", 0, 0, axis_index_groups=groups)


def swap_cores(value):
    return lax.ppermute(value, "vox", [(v, v ^ 1) for v in range(VOX)])


def add_up(parts):
    return jnp.sum(parts.astype(F32), axis=0)


def tree(own, series):
    core = (lax.axis_index("vox") & 1).astype(jnp.int32).reshape(1)
    other = partner(own, 1)
    turned, own_parts = self_gram(own)
    far_own = partner(own, 3)
    far_other = partner(other, 3)
    own_rows = add_up(exchange(own_parts))
    other_rows = partner(own_rows, 1)
    cross_rows = add_up(exchange(cross_gram(turned, other)))
    rows = jnp.concatenate([own_rows, other_rows, cross_rows], axis=0)
    mine = same_core(rows)
    theirs = swap_cores(mine)
    w, left, parts = full_merge(core, mine, theirs, own, other, far_own, far_other)
    parts = exchange(parts)
    far_w = partner(w, 3)
    deep_left = partner(left, 4)
    deep_right = partner(left, 7)
    cross = exchange(cross_rows_of(parts, far_w))
    right = mix(far_own, far_other, far_w)
    w, turned = plain_merge(cross.reshape(N, N), left, right)

    parts = project(turned, deep_left, deep_right)
    parts = exchange(parts)
    deep_w = partner(w, 4)
    cross = exchange(cross_rows_of(parts, deep_w))
    right = mix(deep_left, deep_right, deep_w)
    parts = last_merge(cross.reshape(N, N), turned, right, series)
    return add_up(exchange(parts))


def local(group_basis, timeseries):
    return tree(group_basis[0], timeseries[0])[None]


def solution(mesh):
    return jax.shard_map(
        local,
        mesh=mesh,
        in_specs=(P("grp", "vox", None), P("grp", "vox", None)),
        out_specs=P("grp", "vox", None),
        check_vma=False,
    )
```
